32 devices in a mesh: cell: 8 (over z, core), rays: 4 (over y, x).
Axes of the slice: x: 2, y: 2, z: 4, core: 2. Of those that a mesh axis runs over, the one named last changes fastest.
Arguments:
- ray_code: bfloat16 [1024, 8, 256], P('rays', 'cell'), may hold values from -6 to 6
- entry_index: int32 [1024, 8], P('rays', 'cell'), may hold values from 0 to 120
- sample_count: int32 [1024, 8], P('rays', 'cell'), may hold values from 0 to 8
- step_length: float32 [1024, 8], P('rays', 'cell'), may hold values from 0.0001 to 0.75
- positions: bfloat16 [8, 128, 256], P('cell'), may hold values from -6 to 6
- w_first: bfloat16 [8, 256, 256], P('cell'), may hold values from -0.375 to 0.375
- w_second: float32 [8, 256, 256], P('cell'), may hold values from -0.375 to 0.375
- w_density: bfloat16 [8, 256], P('cell'), may hold values from -0.375 to 0.375
- w_feature: float32 [8, 256, 768], P('cell'), may hold values from -0.375 to 0.375
- mean_second: float32 [8, 256, 256], P('cell'), may hold values from -2 to 2
- square_second: float32 [8, 256, 256], P('cell'), may hold values from 0.0005 to 0.002
- mean_feature: float32 [8, 256, 768], P('cell'), may hold values from -2 to 2
- square_feature: float32 [8, 256, 768], P('cell'), may hold values from 0.0005 to 0.002
- target_color: bfloat16 [1024, 768], P('rays'), may hold values from -6 to 6
Outputs:
- rendered: bfloat16 [1024, 768], P('rays', 'cell')
- depth_grad: float32 [1024, 8], P('rays', 'cell')
- update_second: bfloat16 [8, 256, 256], P('cell')
- update_feature: bfloat16 [8, 256, 768], P('cell')
The draws below stay inside these ranges and needn't reach their ends.
Inputs may be any that keep to these rules, and one draw needn't show every extreme that they name: Samples of a ray in a cell use the table rows entry_index to entry_index + 7. Slots from sample_count on lie outside the cell.
All inputs are finite; a program needn't handle non-finite values.
Results may differ from the reference program's by a relative error of at most 0.0075.
Values may be sent and summed in bfloat16 or wider, within the bound.
No kernel may reach another device: no remote copies, remote signals or barrier semaphores. Data moves between devices by JAX's collectives and lax.ppermute only.
A program may use at most 64 MiB of HBM per device.

```python
import math
import jax
import jax.numpy as jnp
from jax import lax

W = 256
F = 768
SAMPLES = 8
POSITIONS = 128
REGION_COUNT = 8
BEAM_COUNT = 1024


def draw_step_length(key, part):
    stochastic_seeds = jax.random.split(jax.random.fold_in(key, 17), 4)
    low_rate, high_rate = (math.log(0.0003), math.log(0.3))
    beam_proportion = jnp.exp(jax.random.uniform(stochastic_seeds[0], (BEAM_COUNT, 1), jnp.float32, low_rate, high_rate))
    approximate_guess = jnp.exp(jax.random.uniform(stochastic_seeds[1], (BEAM_COUNT, REGION_COUNT), jnp.float32, math.log(0.5), math.log(2.0)))
    sample_batch = jax.random.uniform(stochastic_seeds[2], (BEAM_COUNT, REGION_COUNT), jnp.float32) < 0.08
    additional_summand = jax.random.uniform(stochastic_seeds[3], (BEAM_COUNT, REGION_COUNT), jnp.float32, 0.04, 0.12)
    return beam_proportion * approximate_guess + jnp.where(sample_batch, additional_summand, 0.0)


def draw_target_color(key, part):
    color_seeds = jax.random.split(jax.random.fold_in(key, 29), 1)
    teacher = jax.random.normal(color_seeds[0], (BEAM_COUNT, F), jnp.float32)
    return jnp.clip(teacher, -6.0, 6.0).astype(jnp.bfloat16)


def touch_ends(drawn, key, low, high):
    spot = [jax.random.randint(jax.random.fold_in(key, axis), (), 0, length) for axis, length in enumerate(drawn.shape)]
    widest = drawn.shape.index(max(drawn.shape))
    next_to = spot[:widest] + [(spot[widest] + 1) % drawn.shape[widest]] + spot[widest + 1:]
    return drawn.at[tuple(spot)].set(low).at[tuple(next_to)].set(high)


def steps_of(stream_key, dims, cuts, low, top_value):
    def one(axis_at, parts):
        heights = jax.random.uniform(jax.random.fold_in(jax.random.fold_in(stream_key, 6), axis_at), (parts,), jnp.float32, low / len(cuts), top_value / len(cuts))
        return jnp.repeat(jnp.exp(heights), dims[axis_at] // parts).reshape((-1,) + (1,) * (len(dims) - axis_at - 1))

    level = one(*cuts[0])
    for cut in cuts[1:]:
        level = level * one(*cut)
    return level


def noise(stream_key, shape, deviation, limit, cuts=(), kind=jnp.bfloat16):
    result = deviation * jax.random.normal(stream_key, shape, jnp.float32)
    if cuts:
        result = result * steps_of(stream_key, shape, cuts, -0.22, 0.18)
    return jnp.clip(result, -limit, limit).astype(kind)


def setup_inputs(seed: int = 0) -> dict:
    key_of = jax.random.split(jax.random.key(seed), 15)
    return {
        "ray_code": noise(key_of[0], (BEAM_COUNT, REGION_COUNT, W), 1.0, 6.0, ((0, 4), (1, 8))),
        "entry_index": touch_ends(jax.random.randint(key_of[1], (BEAM_COUNT, REGION_COUNT), 0, POSITIONS - SAMPLES + 1), jax.random.fold_in(key_of[1], 1), 0, POSITIONS - SAMPLES).astype(jnp.int32),
        "sample_count": touch_ends(jax.random.randint(key_of[2], (BEAM_COUNT, REGION_COUNT), 0, SAMPLES + 1), jax.random.fold_in(key_of[2], 1), 0, SAMPLES).astype(jnp.int32),
        "step_length": draw_step_length(jax.random.fold_in(key_of[14], 71), 0),
        "positions": noise(key_of[4], (REGION_COUNT, POSITIONS, W), 1.0, 6.0, ((0, 8),)),
        "w_first": noise(key_of[5], (REGION_COUNT, W, W), W ** -0.5, 0.375, ((0, 8),)),
        "w_second": noise(key_of[6], (REGION_COUNT, W, W), W ** -0.5, 0.375, ((0, 8),), jnp.float32),
        "w_density": noise(key_of[7], (REGION_COUNT, W), W ** -0.5, 0.375, ((0, 8),)),
        "w_feature": noise(key_of[8], (REGION_COUNT, W, F), W ** -0.5, 0.375, ((0, 8),), jnp.float32),
        "mean_second": noise(key_of[9], (REGION_COUNT, W, W), 0.3, 2.0, ((0, 8),), jnp.float32),
        "square_second": jnp.clip(jnp.exp(math.log(0.002) - 1.3862944 * jax.random.uniform(key_of[10], (REGION_COUNT, W, W), jnp.float32) ** steps_of(key_of[10], (REGION_COUNT, W, W), ((0, 8),), -0.2, 0.2)), 0.0005, 0.002),
        "mean_feature": noise(key_of[11], (REGION_COUNT, W, F), 0.3, 2.0, ((0, 8),), jnp.float32),
        "square_feature": jnp.clip(jnp.exp(math.log(0.002) - 1.3862944 * jax.random.uniform(key_of[12], (REGION_COUNT, W, F), jnp.float32) ** steps_of(key_of[12], (REGION_COUNT, W, F), ((0, 8),), -0.2, 0.2)), 0.0005, 0.002),
        "target_color": draw_target_color(jax.random.fold_in(key_of[14], 71), 0),
    }


beta_first = 0.9
beta_second = 0.999
bias_first = 0.19
bias_second = 0.001999
adam_floor = 1e-08
mean_floor = 1e-06

def cell_forward(ray_feat, place_table, entry_index, sample_count, step_length, w_first, w_second, w_density, w_feature):
    ray_rows = ray_feat.shape[0]
    offsets = jnp.arange(SAMPLES, dtype=jnp.int32)
    sample_spot = entry_index[:, None].astype(jnp.int32) + offsets[None, :]
    table_slot = jnp.arange(place_table.shape[0], dtype=jnp.int32)
    one_hot = (sample_spot.reshape(-1, 1) == table_slot[None, :]).astype(jnp.bfloat16)
    placed = jnp.dot(one_hot, place_table, preferred_element_type=jnp.float32)
    inputs = (placed.reshape(ray_rows, SAMPLES, -1) + ray_feat[:, None, :].astype(jnp.float32)).astype(jnp.bfloat16)
    inputs = inputs.reshape(ray_rows * SAMPLES, -1)
    hidden_one = jax.nn.relu(jnp.dot(inputs, w_first, preferred_element_type=jnp.float32)).astype(jnp.bfloat16)
    before = jnp.dot(hidden_one, w_second.astype(jnp.bfloat16), preferred_element_type=jnp.float32)
    hidden_two = jax.nn.relu(before).astype(jnp.bfloat16)
    feature = jnp.dot(hidden_two, w_feature.astype(jnp.bfloat16), preferred_element_type=jnp.float32)
    density_logit = jnp.dot(hidden_two, w_density, preferred_element_type=jnp.float32)
    inside = (offsets[None, :] < sample_count[:, None]).astype(jnp.float32)
    travel = step_length[:, None] * inside
    depth_step = jax.nn.softplus(density_logit).reshape(ray_rows, SAMPLES) * travel
    return (hidden_one, before, hidden_two, feature, density_logit, travel, depth_step)

def composite(depth_step, feature_cube):
    ahead_depth = jnp.cumsum(depth_step, axis=1) - depth_step
    weight = jnp.exp(-ahead_depth) * (1.0 - jnp.exp(-depth_step))
    partial_value = jnp.einsum('rs,rsf->rf', weight, feature_cube)
    return (partial_value, lax.optimization_barrier(jnp.sum(depth_step, axis=1)))

def cell_backward(stored, w_density, w_feature, grad_part, grad_depth):
    hidden_one, before, hidden_two, feature, density_logit, travel, depth_step = stored
    ray_rows = depth_step.shape[0]
    feature_cube = feature.reshape(ray_rows, SAMPLES, -1)
    _, pullback = jax.vjp(composite, depth_step, feature_cube)
    grad_step, grad_cube = pullback((grad_part, grad_depth))
    grad_rows = grad_cube.reshape(ray_rows * SAMPLES, -1).astype(jnp.bfloat16)
    grad_feature = jnp.dot(hidden_two.T, grad_rows, preferred_element_type=jnp.float32)
    grad_logit = (grad_step * travel).reshape(-1) * jax.nn.sigmoid(density_logit)
    grad_hidden = jnp.dot(grad_rows, w_feature.astype(jnp.bfloat16).T, preferred_element_type=jnp.float32)
    grad_hidden = grad_hidden + grad_logit[:, None] * w_density.astype(jnp.float32)[None, :]
    grad_before = jnp.where(before > 0, grad_hidden, 0.0).astype(jnp.bfloat16)
    grad_second = jnp.dot(hidden_one.T, grad_before, preferred_element_type=jnp.float32)
    return (grad_second, grad_feature)

def adam_update(gradient, mean_moment, square_moment, rescale):
    unit_grad = gradient * rescale
    mean_new = beta_first * mean_moment + (1.0 - beta_first) * unit_grad
    square_new = beta_second * square_moment + (1.0 - beta_second) * unit_grad * unit_grad
    return (mean_new / bias_first / (jnp.sqrt(square_new / bias_second) + adam_floor)).astype(jnp.bfloat16)

def reference(ray_code, entry_index, sample_count, step_length, positions, w_first, w_second, w_density, w_feature, mean_second, square_second, mean_feature, square_feature, target_color):
    per_cell = (jnp.swapaxes(ray_code, 0, 1), positions, entry_index.T, sample_count.T, step_length.T, w_first, w_second, w_density, w_feature)

    def forward(cell_items):
        stored = cell_forward(cell_items[0], cell_items[1], cell_items[2], cell_items[3], cell_items[4], cell_items[5], cell_items[6], cell_items[7], cell_items[8])
        ray_rows = cell_items[0].shape[0]
        return composite(stored[6], stored[3].reshape(ray_rows, SAMPLES, -1))
    partials, depths = lax.map(forward, per_cell)
    ahead_depth = jnp.cumsum(depths, axis=0) - depths
    transmit = jnp.exp(-ahead_depth)
    composite_full = lax.optimization_barrier(jnp.sum(transmit[:, :, None] * partials, axis=0))
    residual = composite_full - target_color.astype(jnp.float32)
    bright = transmit * lax.optimization_barrier(jnp.sum(partials * residual[None], axis=2))
    later_sum = lax.optimization_barrier(jnp.sum(bright, axis=0))[None] - jnp.cumsum(bright, axis=0)
    grad_parts = transmit[:, :, None] * residual[None]

    def backward(cell_items):
        stored = cell_forward(cell_items[0], cell_items[1], cell_items[2], cell_items[3], cell_items[4], cell_items[5], cell_items[6], cell_items[7], cell_items[8])
        return cell_backward(stored, cell_items[7], cell_items[8], cell_items[9], -cell_items[10])
    grads_second, grads_feature = lax.map(backward, per_cell + (grad_parts, later_sum))
    square_sum = jnp.sum(grads_second * grads_second) + jnp.sum(grads_feature * grads_feature)
    entry_total = grads_second.size + grads_feature.size
    rescale = lax.rsqrt(square_sum / entry_total + mean_floor)
    update_second = adam_update(grads_second, mean_second, square_second, rescale)
    update_feature = adam_update(grads_feature, mean_feature, square_feature, rescale)
    depth_grad = -later_sum.T
    return (composite_full.astype(jnp.bfloat16), depth_grad, update_second, update_feature)
```

```python
import functools

import jax
import jax.numpy as jnp
from jax import lax
from jax.experimental import pallas as pl
from jax.experimental.pallas import tpu as pltpu
from jax.sharding import PartitionSpec as P


SAMPLES = 8
LANES = 128

beta_first = 0.9
beta_second = 0.999
bias_first = 0.19
bias_second = 0.001999
adam_floor = 1e-08
mean_floor = 1e-06

bf16 = jnp.bfloat16
f32 = jnp.float32

NN = (((1,), (0,)), ((), ()))
NT = (((1,), (1,)), ((), ()))


def mm(a, b, dims=NN):
    return lax.dot_general(a, b, dims, preferred_element_type=f32)


def split_high_low(value):
    high = value.astype(bf16)
    return high, (value - high.astype(f32)).astype(bf16)


def kernel_call(body, outs, scratch=(), name=None, limit=8):
    def call(*args):
        return pl.pallas_call(
            body,
            out_shape=tuple(jax.ShapeDtypeStruct(s, d) for s, d in outs),
            in_specs=[pl.BlockSpec(memory_space=pltpu.VMEM)] * len(args),
            out_specs=tuple(pl.BlockSpec(memory_space=pltpu.VMEM) for _ in outs),
            scratch_shapes=list(scratch),
            compiler_params=pltpu.CompilerParams(vmem_limit_bytes=limit << 20),
            name=name,
        )(*args)

    return call


def bit_of(cell, level):
    return lax.rem(lax.div(cell, 1 << level), 2)


def row_offset(cell, level, rays):
    start = jnp.int32(0)
    for lower in range(level):
        start = start + bit_of(cell, lower) * (rays >> (lower + 1))
    return start


def low_start(cell, level):
    return lax.div(cell, 2 << level) * (2 << level)


def depth_between(depths, first, last):
    place = lax.broadcasted_iota(jnp.int32, depths.shape, 0)
    inside = jnp.logical_and(place >= first, place < last)
    return jnp.sum(jnp.where(inside, depths, 0.0), axis=0, keepdims=True)


def to_column(row):
    return jnp.transpose(jnp.broadcast_to(row, (LANES, row.shape[1])))


def wide(column, width):
    return jnp.concatenate([column] * (width // LANES), axis=1)


def forward_body(
    rays,
    entry_ref,
    count_ref,
    step_ref,
    code_ref,
    table_ref,
    w_first_ref,
    w_second_ref,
    w_density_ref,
    w_feature_ref,
    keep_ref,
    send_ref,
    depth_ref,
    hidden_one_ref,
    hidden_two_ref,
    mean_hidden_ref,
    w_feature_out_ref,
    logit_ref,
    partial_ref,
):
    cell = lax.axis_index("cell")
    w_first_t = jnp.transpose(w_first_ref[...].astype(f32)).astype(bf16)
    w_second_t = jnp.transpose(w_second_ref[...]).astype(bf16)
    rows = table_ref.shape[0]
    table = jnp.concatenate(split_high_low(mm(w_first_t, table_ref[...], NT)), axis=1)
    code = mm(w_first_t, code_ref[...], NT)
    density = jnp.transpose(
        jnp.broadcast_to(w_density_ref[...].astype(f32), (LANES, w_density_ref.shape[1]))
    )
    density = wide(density, rays)
    entry = entry_ref[...]
    slot = lax.broadcasted_iota(jnp.int32, (rows, rays), 0)
    for k in range(SAMPLES):
        cols = pl.ds(k * rays, rays)
        hot = (slot == entry + k).astype(f32).astype(bf16)
        hidden_one = jnp.maximum(mm(table, jnp.concatenate([hot, hot], axis=0)) + code, 0.0)
        hidden_one = hidden_one.astype(bf16)
        hidden_one_ref[:, cols] = hidden_one
        hidden_two = jnp.maximum(mm(w_second_t, hidden_one), 0.0).astype(bf16)
        hidden_two_ref[:, cols] = hidden_two
        logit_ref[k : k + 1, :] = jnp.sum(hidden_two.astype(f32) * density, axis=0, keepdims=True)
    depth_steps, weights, _ = slot_scalars(logit_ref[...], step_ref[...], count_ref[...])
    mean_hidden = jnp.zeros(mean_hidden_ref.shape, f32)
    for k in range(SAMPLES):
        mean_hidden += weights[k] * hidden_two_ref[:, pl.ds(k * rays, rays)].astype(f32)
    mean_hidden_ref[...] = mean_hidden
    w_feature = w_feature_ref[...].astype(bf16)
    w_feature_out_ref[...] = w_feature
    high, low = split_high_low(jnp.transpose(mean_hidden))
    partial_ref[...] = mm(high, w_feature) + mm(low, w_feature)
    half = keep_ref.shape[0]
    mine = lax.rem(cell, 2)
    keep_ref[...] = partial_ref[pl.ds(pl.multiple_of(mine * half, half), half), :].astype(bf16)
    other = rays - half
    send_ref[...] = partial_ref[
        pl.ds(pl.multiple_of((1 - mine) * other, send_ref.shape[0]), send_ref.shape[0]), :
    ].astype(bf16)
    place = lax.broadcasted_iota(jnp.int32, depth_ref.shape, 0)
    total = functools.reduce(lambda a, b: a + b, depth_steps)
    depth_ref[...] = jnp.where(place == cell, jnp.broadcast_to(total, depth_ref.shape), 0.0)


def slot_scalars(logit, step_length, count):
    soft = jnp.maximum(logit, 0.0) + jnp.log1p(jnp.exp(-jnp.abs(logit)))
    depth_steps, weights, behinds = [], [], []
    ahead = jnp.zeros_like(step_length)
    for k in range(SAMPLES):
        travel = jnp.where(k < count, step_length, 0.0)
        depth = soft[k : k + 1, :] * travel
        weights.append(jnp.exp(-ahead) * (1.0 - jnp.exp(-depth)))
        ahead = ahead + depth
        behinds.append(jnp.exp(-ahead))
        depth_steps.append(depth)
    return depth_steps, weights, behinds


def joined(cell, level, rays, mine, theirs, depths, column_ref):
    count = mine.shape[0]
    start = low_start(cell, level)
    fade = jnp.exp(-depth_between(depths, start, start + (1 << level)))
    column_ref[...] = to_column(fade)
    offset = row_offset(cell, level + 1 if count < (rays >> level) else level, rays)
    fade = column_ref[pl.ds(pl.multiple_of(offset, count), count), :]
    is_low = bit_of(cell, level) == 0
    own = wide(jnp.where(is_low, 1.0, fade), mine.shape[1])
    other = wide(jnp.where(is_low, fade, 1.0), mine.shape[1])
    return own * mine.astype(f32) + other * theirs.astype(f32)


def up_body(
    level, rays, mine_ref, theirs_ref, depth_ref, depth_in_ref, keep_ref, send_ref, depth_out_ref,
    column_ref, joined_ref,
):
    cell = lax.axis_index("cell")
    depths = depth_ref[...] + depth_in_ref[...]
    depth_out_ref[...] = depths
    value = joined(cell, level, rays, mine_ref[...], theirs_ref[...], depths, column_ref)
    count, half = value.shape[0], keep_ref.shape[0]
    if half == count:
        keep_ref[...] = value.astype(bf16)
        send_ref[...] = value.astype(bf16)
    else:
        joined_ref[...] = value
        mine = bit_of(cell, level + 1)
        keep_ref[...] = joined_ref[pl.ds(pl.multiple_of(mine * half, half), half), :].astype(bf16)
        send_ref[...] = joined_ref[
            pl.ds(pl.multiple_of((1 - mine) * half, half), half), :
        ].astype(bf16)


def later_light(cell, level, rays, residual, mine, theirs, depths, column_ref):
    count = residual.shape[0]
    high = jnp.where(bit_of(cell, level) == 0, theirs.astype(f32), mine.astype(f32))
    dots = jnp.sum(high * residual, axis=1, keepdims=True)
    offset = row_offset(cell, level if count == (rays >> level) else level + 1, rays)
    column_ref[...] = jnp.zeros_like(column_ref)
    column_ref[pl.ds(pl.multiple_of(offset, count), count), :] = jnp.broadcast_to(
        dots, (count, LANES)
    )
    row = jnp.transpose(column_ref[...])[0:1, :]
    transmit = jnp.exp(-depth_between(depths, 0, low_start(cell, level) + (1 << level)))
    return transmit * row


def share_light(cell, level, later, light, own_ref, their_ref):
    is_low = bit_of(cell, level) == 0
    own_ref[...] = jnp.broadcast_to(later + jnp.where(is_low, light, 0.0), own_ref.shape)
    their_ref[...] = jnp.broadcast_to(later + jnp.where(is_low, 0.0, light), their_ref.shape)


def top_body(
    level, rays, mine_ref, theirs_ref, depth_ref, depth_in_ref, under_mine_ref, under_theirs_ref,
    target_ref, color_ref, later_ref, later_send_ref, depth_out_ref, column_ref,
):
    cell = lax.axis_index("cell")
    depths = depth_ref[...] + depth_in_ref[...]
    depth_out_ref[...] = depths
    mine, theirs = mine_ref[...], theirs_ref[...]
    color = joined(cell, level, rays, mine, theirs, depths, column_ref).astype(bf16)
    color_ref[...] = color
    count = color.shape[0]
    offset = pl.multiple_of(row_offset(cell, level, rays), count)
    residual = color.astype(f32) - target_ref[pl.ds(offset, count), :].astype(f32)
    light = later_light(cell, level, rays, residual, mine, theirs, depths, column_ref)
    later = jnp.where(bit_of(cell, level) == 0, light, 0.0)
    light = later_light(
        cell, level - 1, rays, residual, under_mine_ref[...], under_theirs_ref[...], depths,
        column_ref,
    )
    share_light(cell, level - 1, later, light, later_ref, later_send_ref)


def assembled(cell, level, mine, theirs, out_ref):
    count = mine.shape[0]
    bit = bit_of(cell, level)
    out_ref[pl.ds(pl.multiple_of(bit * count, count), count), :] = mine
    out_ref[pl.ds(pl.multiple_of((1 - bit) * count, count), count), :] = theirs


def down_body(
    level, rays, color_ref, color_in_ref, later_ref, later_in_ref, depth_ref, mine_ref, theirs_ref,
    target_ref, color_out_ref, later_out_ref, later_send_ref, column_ref,
):
    cell = lax.axis_index("cell")
    assembled(cell, level + 1, color_ref[...], color_in_ref[...], color_out_ref)
    later = later_ref[0:1, :] + later_in_ref[0:1, :]
    count = color_out_ref.shape[0]
    offset = pl.multiple_of(row_offset(cell, level + 1, rays), count)
    residual = color_out_ref[...].astype(f32) - target_ref[pl.ds(offset, count), :].astype(f32)
    light = later_light(
        cell, level, rays, residual, mine_ref[...], theirs_ref[...], depth_ref[...], column_ref
    )
    share_light(cell, level, later, light, later_out_ref, later_send_ref)


def backward_body(
    rays,
    color_ref,
    color_in_ref,
    later_ref,
    later_in_ref,
    depth_ref,
    target_ref,
    hidden_one_ref,
    hidden_two_ref,
    mean_hidden_ref,
    w_feature_ref,
    logit_ref,
    step_ref,
    count_ref,
    w_density_ref,
    rendered_ref,
    depth_grad_ref,
    first_ref,
    second_ref,
    whole_ref,
):
    cell = lax.axis_index("cell")
    assembled(cell, 0, color_ref[...], color_in_ref[...], whole_ref)
    color = whole_ref[...]
    width = rendered_ref.shape[0]
    place = lax.broadcasted_iota(jnp.int32, (width, color.shape[1]), 0)
    channel = lax.broadcasted_iota(jnp.int32, (width, color.shape[1]), 1)
    chosen = (channel == place + cell * width).astype(f32).astype(bf16)
    rendered_ref[...] = mm(chosen, color, NT).astype(bf16)
    residual = (color.astype(f32) - target_ref[...].astype(f32)).astype(bf16)
    grad_depth = -(later_ref[0:1, :] + later_in_ref[0:1, :])
    depth_grad_ref[...] = grad_depth
    transmit = jnp.exp(-depth_between(depth_ref[...], 0, cell))
    half = first_ref.shape[0]
    features = residual.shape[1]
    grad_feature = mm((mean_hidden_ref[...] * transmit).astype(bf16), residual).astype(bf16)
    first_ref[:, :features] = grad_feature[:half]
    second_ref[:, :features] = grad_feature[half:]
    pulled = mm(w_feature_ref[...], residual, NT) * transmit

    logit = logit_ref[...]
    _, weights, behinds = slot_scalars(logit, step_ref[...], count_ref[...])
    sigmoid = 1.0 / (1.0 + jnp.exp(-logit))
    dots = [
        jnp.sum(hidden_two_ref[:, pl.ds(k * rays, rays)].astype(f32) * pulled, axis=0, keepdims=True)
        for k in range(SAMPLES)
    ]
    later = jnp.zeros_like(grad_depth)
    grad_logits = [None] * SAMPLES
    for k in reversed(range(SAMPLES)):
        grad_step = behinds[k] * dots[k] - later + grad_depth
        later = later + weights[k] * dots[k]
        travel = jnp.where(k < count_ref[...], step_ref[...], 0.0)
        grad_logits[k] = grad_step * travel * sigmoid[k : k + 1, :]
    density = jnp.transpose(
        jnp.broadcast_to(w_density_ref[...].astype(f32), (LANES, w_density_ref.shape[1]))
    )
    density = wide(density, rays)
    grad_second = jnp.zeros((hidden_one_ref.shape[0], hidden_one_ref.shape[0]), f32)
    for k in range(SAMPLES):
        cols = pl.ds(k * rays, rays)
        grad_hidden = weights[k] * pulled + grad_logits[k] * density
        grad_before = jnp.where(hidden_two_ref[:, cols].astype(f32) > 0, grad_hidden, 0.0)
        grad_second += mm(hidden_one_ref[:, cols], grad_before.astype(bf16), NT)
    grad_second = grad_second.astype(bf16)
    first_ref[:, features:] = grad_second[:half]
    second_ref[:, features:] = grad_second[half:]


def add_body(*refs):
    count = len(refs) // 3
    for a, b, out in zip(refs[:count], refs[count : 2 * count], refs[2 * count :]):
        out[...] = (a[...].astype(f32) + b[...].astype(f32)).astype(out.dtype)


def square_body(first_ref, second_ref, first_in_ref, second_in_ref, first_out, second_out, sum_ref):
    total = jnp.zeros((1, first_ref.shape[1]), f32)
    for a, b, out in (
        (first_ref, first_in_ref, first_out),
        (second_ref, second_in_ref, second_out),
    ):
        value = a[...].astype(f32) + b[...].astype(f32)
        out[...] = value
        total += jnp.sum(value * value, axis=0, keepdims=True)
    sum_ref[...] = jnp.broadcast_to(jnp.sum(total, axis=1, keepdims=True), sum_ref.shape)


def adam_of(gradient, mean_moment, square_moment, rescale):
    unit_grad = gradient * rescale
    mean_new = beta_first * mean_moment + (1.0 - beta_first) * unit_grad
    square_new = beta_second * square_moment + (1.0 - beta_second) * unit_grad * unit_grad
    return (mean_new / bias_first / (jnp.sqrt(square_new / bias_second) + adam_floor)).astype(bf16)


def adam_body(
    entries, sum_ref, sum_in_ref, first_ref, second_ref, mean_second_ref, square_second_ref,
    mean_feature_ref, square_feature_ref, update_second_ref, update_feature_ref,
):
    total = sum_ref[0:1, :] + sum_in_ref[0:1, :]
    rescale = lax.rsqrt(total / entries + mean_floor)
    half = first_ref.shape[0]
    features = mean_feature_ref.shape[1]
    for ref, start in ((first_ref, 0), (second_ref, half)):
        rows = pl.ds(start, half)
        update_feature_ref[rows, :] = adam_of(
            ref[:, :features], mean_feature_ref[rows, :], square_feature_ref[rows, :],
            wide(rescale, features),
        )
        update_second_ref[rows, :] = adam_of(
            ref[:, features:], mean_second_ref[rows, :], square_second_ref[rows, :],
            wide(rescale, mean_second_ref.shape[1]),
        )


def swap(value, axis, bit):
    count = lax.axis_size(axis)
    return lax.ppermute(value, axis, [(i, i ^ (1 << bit)) for i in range(count)])


def on_device(
    ray_code,
    entry_index,
    sample_count,
    step_length,
    positions,
    w_first,
    w_second,
    w_density,
    w_feature,
    mean_second,
    square_second,
    mean_feature,
    square_feature,
    target_color,
):
    rays, _, hidden = ray_code.shape
    features = w_feature.shape[2]
    cells = lax.axis_size("cell")
    groups = lax.axis_size("rays")
    levels = cells.bit_length() - 1
    spread = groups.bit_length() - 1
    entry, count, step = entry_index.T, sample_count.T, step_length.T
    column = pltpu.VMEM((rays, LANES), f32)

    half = rays // 2
    keep, send, depths, hidden_one, hidden_two, mean_hidden, w_feature_b, logit = kernel_call(
        functools.partial(forward_body, rays),
        [
            ((half, features), bf16),
            ((half, features), bf16),
            ((cells, rays), f32),
            ((hidden, SAMPLES * rays), bf16),
            ((hidden, SAMPLES * rays), bf16),
            ((hidden, rays), f32),
            ((hidden, features), bf16),
            ((SAMPLES, rays), f32),
        ],
        [pltpu.VMEM((rays, features), f32)],
        "forward",
        16,
    )(entry, count, step, ray_code[:, 0, :], positions[0], w_first[0], w_second[0], w_density,
      w_feature[0])

    held = []
    for level in range(levels - 1):
        theirs = swap(send, "cell", level)
        depths_in = swap(depths, "cell", level)
        held.append((keep, theirs))
        rows = keep.shape[0]
        next_rows = rows if level == levels - 2 else rows // 2
        keep, send, depths = kernel_call(
            functools.partial(up_body, level, rays),
            [((next_rows, features), bf16), ((next_rows, features), bf16), ((cells, rays), f32)],
            [column, pltpu.VMEM((rows, features), f32)],
            f"up_{level}",
        )(keep, theirs, depths, depths_in)

    theirs = swap(send, "cell", levels - 1)
    depths_in = swap(depths, "cell", levels - 1)
    color, later, later_send, depths = kernel_call(
        functools.partial(top_body, levels - 1, rays),
        [(keep.shape, bf16), ((8, rays), f32), ((8, rays), f32), ((cells, rays), f32)],
        [column],
        "top",
    )(keep, theirs, depths, depths_in, *held[-1], target_color)

    for level in reversed(range(levels - 2)):
        color_in = swap(color, "cell", level + 1)
        later_in = swap(later_send, "cell", level + 1)
        color, later, later_send = kernel_call(
            functools.partial(down_body, level, rays),
            [((2 * color.shape[0], features), bf16), ((8, rays), f32), ((8, rays), f32)],
            [column],
            f"down_{level}",
        )(color, color_in, later, later_in, depths, *held[level], target_color)

    color_in = swap(color, "cell", 0)
    later_in = swap(later_send, "cell", 0)
    joint = (hidden // 2, features + hidden)
    rendered, depth_grad, first, second = kernel_call(
        functools.partial(backward_body, rays),
        [((features // cells, rays), bf16), ((1, rays), f32), (joint, bf16), (joint, bf16)],
        [pltpu.VMEM((rays, features), bf16)],
        "backward",
        16,
    )(color, color_in, later, later_in, depths, target_color, hidden_one, hidden_two, mean_hidden,
      w_feature_b, logit, step, count, w_density)

    for turn in range(spread):
        first_in = swap(first, "rays", turn)
        second_in = swap(second, "rays", (turn + 1) % spread)
        if turn < spread - 1:
            first, second = kernel_call(add_body, [(joint, bf16), (joint, bf16)], (), "add")(
                first, second, first_in, second_in
            )
        else:
            first, second, total = kernel_call(
                square_body, [(joint, f32), (joint, f32), ((8, LANES), f32)], (), "square"
            )(first, second, first_in, second_in)

    for level in range(levels):
        total_in = swap(total, "cell", level)
        if level < levels - 1:
            total = total + total_in

    entries = cells * (hidden * features + hidden * hidden)
    update_second, update_feature = kernel_call(
        functools.partial(adam_body, entries),
        [((hidden, hidden), bf16), ((hidden, features), bf16)],
        (),
        "adam",
    )(total, total_in, first, second, mean_second[0], square_second[0], mean_feature[0],
      square_feature[0])
    return (rendered.T, depth_grad.T, update_second[None], update_feature[None])


def solution(mesh):
    in_specs = (
        P("rays", "cell", None),
        P("rays", "cell"),
        P("rays", "cell"),
        P("rays", "cell"),
        P("cell", None, None),
        P("cell", None, None),
        P("cell", None, None),
        P("cell", None),
        P("cell", None, None),
        P("cell", None, None),
        P("cell", None, None),
        P("cell", None, None),
        P("cell", None, None),
        P("rays", None),
    )
    out_specs = (P("rays", "cell"), P("rays", "cell"), P("cell", None, None), P("cell", None, None))
    return jax.shard_map(
        on_device, mesh=mesh, in_specs=in_specs, out_specs=out_specs, check_vma=False
    )
```

```python
import functools

import jax
import jax.numpy as jnp
from jax import lax
from jax.experimental import pallas as pl
from jax.experimental.pallas import tpu as pltpu
from jax.sharding import PartitionSpec as P


SAMPLES = 8
LANES = 128

beta_first = 0.9
beta_second = 0.999
bias_first = 0.19
bias_second = 0.001999
adam_floor = 1e-08
mean_floor = 1e-06

bf16 = jnp.bfloat16
f32 = jnp.float32

NN = (((1,), (0,)), ((), ()))
NT = (((1,), (1,)), ((), ()))


def mm(a, b, dims=NN):
    return lax.dot_general(a, b, dims, preferred_element_type=f32)


def split_high_low(value):
    high = value.astype(bf16)
    return high, (value - high.astype(f32)).astype(bf16)


def kernel_call(body, outs, scratch=(), name=None, limit=8, space=pltpu.VMEM):
    def call(*args):
        if space is pltpu.HBM:
            args = [pltpu.with_memory_space_constraint(arg, pltpu.HBM) for arg in args]
        return pl.pallas_call(
            body,
            out_shape=tuple(jax.ShapeDtypeStruct(s, d) for s, d in outs),
            in_specs=[pl.BlockSpec(memory_space=space)] * len(args),
            out_specs=tuple(pl.BlockSpec(memory_space=pltpu.VMEM) for _ in outs),
            scratch_shapes=list(scratch),
            compiler_params=pltpu.CompilerParams(vmem_limit_bytes=limit << 20),
            name=name,
        )(*args)

    return call


def bit_of(cell, level):
    return lax.rem(lax.div(cell, 1 << level), 2)


def row_offset(cell, level, rays):
    start = jnp.int32(0)
    for lower in range(level):
        start = start + bit_of(cell, lower) * (rays >> (lower + 1))
    return start


def low_start(cell, level):
    return lax.div(cell, 2 << level) * (2 << level)


def depth_between(depths, first, last):
    place = lax.broadcasted_iota(jnp.int32, depths.shape, 0)
    inside = jnp.logical_and(place >= first, place < last)
    return jnp.sum(jnp.where(inside, depths, 0.0), axis=0, keepdims=True)


def to_column(row):
    return jnp.transpose(jnp.broadcast_to(row, (LANES, row.shape[1])))


def wide(column, width):
    return jnp.concatenate([column] * (width // LANES), axis=1)


def forward_body(
    rays,
    entry_hbm,
    count_hbm,
    step_hbm,
    density_hbm,
    w_first_hbm,
    table_hbm,
    code_hbm,
    w_second_hbm,
    w_feature_hbm,
    keep_ref,
    send_ref,
    depth_ref,
    hidden_one_ref,
    hidden_two_ref,
    mean_hidden_ref,
    w_feature_out_ref,
    logit_ref,
    step_out_ref,
    count_out_ref,
    density_out_ref,
    partial_ref,
    entry_ref,
    w_first_ref,
    table_ref,
    code_ref,
    w_second_ref,
    w_feature_ref,
    done,
):
    cell = lax.axis_index("cell")
    pairs = (
        (w_first_hbm, w_first_ref),
        (table_hbm, table_ref),
        (code_hbm, code_ref),
        (entry_hbm, entry_ref),
        (w_second_hbm, w_second_ref),
        (density_hbm, density_out_ref),
        (count_hbm, count_out_ref),
        (step_hbm, step_out_ref),
        (w_feature_hbm, w_feature_ref),
    )
    copies = [pltpu.make_async_copy(a, b, done.at[i]) for i, (a, b) in enumerate(pairs)]
    for copy in copies:
        copy.start()
    copies[0].wait()
    w_first_t = jnp.transpose(w_first_ref[...].astype(f32)).astype(bf16)
    copies[1].wait()
    rows = table_ref.shape[0]
    table = jnp.concatenate(split_high_low(mm(w_first_t, table_ref[...], NT)), axis=1)
    copies[2].wait()
    code = mm(w_first_t, code_ref[...], NT)
    for copy in copies[3:8]:
        copy.wait()
    w_second_t = jnp.transpose(w_second_ref[...]).astype(bf16)
    density = density_columns(density_out_ref, rays)
    entry = entry_ref[...]
    slot = lax.broadcasted_iota(jnp.int32, (rows, rays), 0)
    for k in range(SAMPLES):
        cols = pl.ds(k * rays, rays)
        hot = (slot == entry + k).astype(f32).astype(bf16)
        hidden_one = jnp.maximum(mm(table, jnp.concatenate([hot, hot], axis=0)) + code, 0.0)
        hidden_one = hidden_one.astype(bf16)
        hidden_one_ref[:, cols] = hidden_one
        hidden_two = jnp.maximum(mm(w_second_t, hidden_one), 0.0).astype(bf16)
        hidden_two_ref[:, cols] = hidden_two
        logit_ref[k : k + 1, :] = jnp.sum(hidden_two.astype(f32) * density, axis=0, keepdims=True)
    depth_steps, weights, _ = slot_scalars(logit_ref[...], step_out_ref[...], count_out_ref[...])
    mean_hidden = jnp.zeros(mean_hidden_ref.shape, f32)
    for k in range(SAMPLES):
        mean_hidden += weights[k] * hidden_two_ref[:, pl.ds(k * rays, rays)].astype(f32)
    mean_hidden_ref[...] = mean_hidden
    copies[8].wait()
    w_feature = w_feature_ref[...].astype(bf16)
    w_feature_out_ref[...] = w_feature
    high, low = split_high_low(jnp.transpose(mean_hidden))
    partial_ref[...] = mm(high, w_feature) + mm(low, w_feature)
    half = keep_ref.shape[0]
    mine = lax.rem(cell, 2)
    keep_ref[...] = partial_ref[pl.ds(pl.multiple_of(mine * half, half), half), :].astype(bf16)
    send_ref[...] = partial_ref[
        pl.ds(pl.multiple_of((1 - mine) * half, half), half), :
    ].astype(bf16)
    place = lax.broadcasted_iota(jnp.int32, depth_ref.shape, 0)
    total = functools.reduce(lambda a, b: a + b, depth_steps)
    depth_ref[...] = jnp.where(place == cell, jnp.broadcast_to(total, depth_ref.shape), 0.0)


def density_columns(density_ref, rays):
    density = density_ref[...].astype(f32)
    return wide(jnp.transpose(jnp.broadcast_to(density, (LANES, density.shape[1]))), rays)


def slot_scalars(logit, step_length, count):
    soft = jnp.maximum(logit, 0.0) + jnp.log1p(jnp.exp(-jnp.abs(logit)))
    depth_steps, weights, behinds = [], [], []
    ahead = jnp.zeros_like(step_length)
    for k in range(SAMPLES):
        travel = jnp.where(k < count, step_length, 0.0)
        depth = soft[k : k + 1, :] * travel
        weights.append(jnp.exp(-ahead) * (1.0 - jnp.exp(-depth)))
        ahead = ahead + depth
        behinds.append(jnp.exp(-ahead))
        depth_steps.append(depth)
    return depth_steps, weights, behinds


def joined(cell, level, rays, mine, theirs, depths, column_ref):
    count = mine.shape[0]
    start = low_start(cell, level)
    fade = jnp.exp(-depth_between(depths, start, start + (1 << level)))
    column_ref[...] = to_column(fade)
    offset = row_offset(cell, level + 1 if count < (rays >> level) else level, rays)
    fade = column_ref[pl.ds(pl.multiple_of(offset, count), count), :]
    is_low = bit_of(cell, level) == 0
    own = wide(jnp.where(is_low, 1.0, fade), mine.shape[1])
    other = wide(jnp.where(is_low, fade, 1.0), mine.shape[1])
    return own * mine.astype(f32) + other * theirs.astype(f32)


def up_body(
    level, rays, mine_ref, theirs_ref, depth_ref, depth_in_ref, keep_ref, send_ref, depth_out_ref,
    column_ref, joined_ref,
):
    cell = lax.axis_index("cell")
    depths = depth_ref[...] + depth_in_ref[...]
    depth_out_ref[...] = depths
    value = joined(cell, level, rays, mine_ref[...], theirs_ref[...], depths, column_ref)
    count, half = value.shape[0], keep_ref.shape[0]
    if half == count:
        keep_ref[...] = value.astype(bf16)
        send_ref[...] = value.astype(bf16)
    else:
        joined_ref[...] = value
        mine = bit_of(cell, level + 1)
        keep_ref[...] = joined_ref[pl.ds(pl.multiple_of(mine * half, half), half), :].astype(bf16)
        send_ref[...] = joined_ref[
            pl.ds(pl.multiple_of((1 - mine) * half, half), half), :
        ].astype(bf16)


def later_light(cell, level, rays, residual, mine, theirs, depths, column_ref):
    count = residual.shape[0]
    high = jnp.where(bit_of(cell, level) == 0, theirs.astype(f32), mine.astype(f32))
    dots = jnp.sum(high * residual, axis=1, keepdims=True)
    offset = row_offset(cell, level if count == (rays >> level) else level + 1, rays)
    column_ref[...] = jnp.zeros_like(column_ref)
    column_ref[pl.ds(pl.multiple_of(offset, count), count), :] = jnp.broadcast_to(
        dots, (count, LANES)
    )
    row = jnp.transpose(column_ref[...])[0:1, :]
    transmit = jnp.exp(-depth_between(depths, 0, low_start(cell, level) + (1 << level)))
    return transmit * row


def share_light(cell, level, later, light, own_ref, their_ref):
    is_low = bit_of(cell, level) == 0
    own_ref[...] = jnp.broadcast_to(later + jnp.where(is_low, light, 0.0), own_ref.shape)
    their_ref[...] = jnp.broadcast_to(later + jnp.where(is_low, 0.0, light), their_ref.shape)


def top_body(
    level, rays, mine_ref, theirs_ref, depth_ref, depth_in_ref, under_mine_ref, under_theirs_ref,
    target_ref, color_ref, later_ref, later_send_ref, depth_out_ref, column_ref,
):
    cell = lax.axis_index("cell")
    depths = depth_ref[...] + depth_in_ref[...]
    depth_out_ref[...] = depths
    mine, theirs = mine_ref[...], theirs_ref[...]
    color = joined(cell, level, rays, mine, theirs, depths, column_ref).astype(bf16)
    color_ref[...] = color
    count = color.shape[0]
    offset = pl.multiple_of(row_offset(cell, level, rays), count)
    residual = color.astype(f32) - target_ref[pl.ds(offset, count), :].astype(f32)
    light = later_light(cell, level, rays, residual, mine, theirs, depths, column_ref)
    later = jnp.where(bit_of(cell, level) == 0, light, 0.0)
    light = later_light(
        cell, level - 1, rays, residual, under_mine_ref[...], under_theirs_ref[...], depths,
        column_ref,
    )
    share_light(cell, level - 1, later, light, later_ref, later_send_ref)


def assembled(cell, level, mine, theirs, out_ref):
    count = mine.shape[0]
    bit = bit_of(cell, level)
    out_ref[pl.ds(pl.multiple_of(bit * count, count), count), :] = mine
    out_ref[pl.ds(pl.multiple_of((1 - bit) * count, count), count), :] = theirs


def down_body(
    level, rays, color_ref, color_in_ref, later_ref, later_in_ref, depth_ref, mine_ref, theirs_ref,
    target_ref, color_out_ref, later_out_ref, later_send_ref, column_ref,
):
    cell = lax.axis_index("cell")
    assembled(cell, level + 1, color_ref[...], color_in_ref[...], color_out_ref)
    later = later_ref[0:1, :] + later_in_ref[0:1, :]
    count = color_out_ref.shape[0]
    offset = pl.multiple_of(row_offset(cell, level + 1, rays), count)
    residual = color_out_ref[...].astype(f32) - target_ref[pl.ds(offset, count), :].astype(f32)
    light = later_light(
        cell, level, rays, residual, mine_ref[...], theirs_ref[...], depth_ref[...], column_ref
    )
    share_light(cell, level, later, light, later_out_ref, later_send_ref)


def feature_body(
    rays,
    color_ref,
    color_in_ref,
    later_ref,
    later_in_ref,
    depth_ref,
    target_ref,
    mean_hidden_ref,
    w_feature_ref,
    whole_ref,
    grad_depth_ref,
    pulled_ref,
    *grad_refs,
):
    cell = lax.axis_index("cell")
    grad_depth_ref[...] = -(later_ref[...] + later_in_ref[...])
    assembled(cell, 0, color_ref[...], color_in_ref[...], whole_ref)
    color = whole_ref[...]
    residual = (color.astype(f32) - target_ref[...].astype(f32)).astype(bf16)
    transmit = jnp.exp(-depth_between(depth_ref[...], 0, cell))
    seen = (mean_hidden_ref[...] * transmit).astype(bf16)
    start = 0
    for ref in grad_refs:
        width = ref.shape[1]
        ref[...] = mm(seen, residual[:, start : start + width]).astype(bf16)
        start += width
    pulled_ref[...] = mm(w_feature_ref[...], residual, NT) * transmit


def output_body(color_ref, grad_depth_ref, rendered_ref, depth_grad_ref):
    cell = lax.axis_index("cell")
    width, channels = rendered_ref.shape[0], color_ref.shape[1]
    place = lax.broadcasted_iota(jnp.int32, (width, channels), 0)
    channel = lax.broadcasted_iota(jnp.int32, (width, channels), 1)
    chosen = (channel == place + cell * width).astype(f32).astype(bf16)
    rendered_ref[...] = mm(chosen, color_ref[...], NT).astype(bf16)
    depth_grad_ref[...] = grad_depth_ref[0:1, :]


def hidden_body(
    rays,
    pulled_ref,
    grad_depth_ref,
    hidden_one_ref,
    hidden_two_ref,
    logit_ref,
    step_ref,
    count_ref,
    density_ref,
    grad_ref,
):
    pulled, grad_depth = pulled_ref[...], grad_depth_ref[0:1, :]
    logit = logit_ref[...]
    _, weights, behinds = slot_scalars(logit, step_ref[...], count_ref[...])
    sigmoid = 1.0 / (1.0 + jnp.exp(-logit))
    dots = [
        jnp.sum(hidden_two_ref[:, pl.ds(k * rays, rays)].astype(f32) * pulled, axis=0, keepdims=True)
        for k in range(SAMPLES)
    ]
    later = jnp.zeros_like(grad_depth)
    grad_logits = [None] * SAMPLES
    for k in reversed(range(SAMPLES)):
        grad_step = behinds[k] * dots[k] - later + grad_depth
        later = later + weights[k] * dots[k]
        travel = jnp.where(k < count_ref[...], step_ref[...], 0.0)
        grad_logits[k] = grad_step * travel * sigmoid[k : k + 1, :]
    density = density_columns(density_ref, rays)
    grad_second = jnp.zeros(grad_ref.shape, f32)
    for k in range(SAMPLES):
        cols = pl.ds(k * rays, rays)
        grad_hidden = weights[k] * pulled + grad_logits[k] * density
        grad_before = jnp.where(hidden_two_ref[:, cols].astype(f32) > 0, grad_hidden, 0.0)
        grad_second += mm(hidden_one_ref[:, cols], grad_before.astype(bf16), NT)
    grad_ref[...] = grad_second.astype(bf16)


def add_body(a_ref, b_ref, out_ref):
    out_ref[...] = (a_ref[...].astype(f32) + b_ref[...].astype(f32)).astype(out_ref.dtype)


def square_body(a_ref, b_ref, *rest):
    *before_ref, out_ref, sum_ref = rest
    value = a_ref[...].astype(f32) + b_ref[...].astype(f32)
    out_ref[...] = value
    total = jnp.sum(jnp.sum(value * value, axis=0, keepdims=True), axis=1, keepdims=True)
    total = jnp.broadcast_to(total, sum_ref.shape)
    sum_ref[...] = total + before_ref[0][...] if before_ref else total


def adam_of(gradient, mean_moment, square_moment, rescale):
    unit_grad = gradient * rescale
    mean_new = beta_first * mean_moment + (1.0 - beta_first) * unit_grad
    square_new = beta_second * square_moment + (1.0 - beta_second) * unit_grad * unit_grad
    return (mean_new / bias_first / (jnp.sqrt(square_new / bias_second) + adam_floor)).astype(bf16)


def adam_body(entries, sum_ref, sum_in_ref, *rest):
    *in_refs, update_second_ref, update_feature_ref = rest
    *grad_refs, mean_second_ref, square_second_ref, mean_feature_ref, square_feature_ref = in_refs
    *feature_refs, second_ref = grad_refs
    rescale = lax.rsqrt((sum_ref[0:1, :] + sum_in_ref[0:1, :]) / entries + mean_floor)
    start = 0
    for ref in feature_refs:
        cols = pl.ds(start, ref.shape[1])
        update_feature_ref[:, cols] = adam_of(
            ref[...], mean_feature_ref[:, cols], square_feature_ref[:, cols],
            wide(rescale, ref.shape[1]),
        )
        start += ref.shape[1]
    update_second_ref[...] = adam_of(
        second_ref[...], mean_second_ref[...], square_second_ref[...],
        wide(rescale, second_ref.shape[1]),
    )


def swap(value, axis, bit):
    count = lax.axis_size(axis)
    return lax.ppermute(value, axis, [(i, i ^ (1 << bit)) for i in range(count)])


def swap_groups(value, turn):
    cells, groups = lax.axis_size("cell"), lax.axis_size("rays")
    spread = groups.bit_length() - 1
    pairs = [
        (c * groups + g, c * groups + (g ^ (1 << ((turn + c) % spread))))
        for c in range(cells)
        for g in range(groups)
    ]
    return lax.ppermute(value, ("cell", "rays"), pairs)


def on_device(
    ray_code,
    entry_index,
    sample_count,
    step_length,
    positions,
    w_first,
    w_second,
    w_density,
    w_feature,
    mean_second,
    square_second,
    mean_feature,
    square_feature,
    target_color,
):
    rays, _, hidden = ray_code.shape
    features = w_feature.shape[2]
    cells = lax.axis_size("cell")
    groups = lax.axis_size("rays")
    levels = cells.bit_length() - 1
    spread = groups.bit_length() - 1
    entry, count, step = entry_index.T, sample_count.T, step_length.T
    column = pltpu.VMEM((rays, LANES), f32)

    half = rays // 2
    (
        keep, send, depths, hidden_one, hidden_two, mean_hidden, w_feature_b, logit, step, count,
        density,
    ) = kernel_call(
        functools.partial(forward_body, rays),
        [
            ((half, features), bf16),
            ((half, features), bf16),
            ((cells, rays), f32),
            ((hidden, SAMPLES * rays), bf16),
            ((hidden, SAMPLES * rays), bf16),
            ((hidden, rays), f32),
            ((hidden, features), bf16),
            ((SAMPLES, rays), f32),
            (step.shape, f32),
            (count.shape, jnp.int32),
            (w_density.shape, bf16),
        ],
        [
            pltpu.VMEM((rays, features), f32),
            pltpu.VMEM(entry.shape, jnp.int32),
            pltpu.VMEM(w_first.shape[1:], bf16),
            pltpu.VMEM(positions.shape[1:], bf16),
            pltpu.VMEM((rays, hidden), bf16),
            pltpu.VMEM(w_second.shape[1:], f32),
            pltpu.VMEM(w_feature.shape[1:], f32),
            pltpu.SemaphoreType.DMA((9,)),
        ],
        "forward",
        16,
        pltpu.HBM,
    )(entry, count, step, w_density, w_first[0], positions[0], ray_code[:, 0, :], w_second[0],
      w_feature[0])

    held = []
    for level in range(levels - 1):
        theirs = swap(send, "cell", level)
        depths_in = swap(depths, "cell", level)
        held.append((keep, theirs))
        rows = keep.shape[0]
        next_rows = rows if level == levels - 2 else rows // 2
        keep, send, depths = kernel_call(
            functools.partial(up_body, level, rays),
            [((next_rows, features), bf16), ((next_rows, features), bf16), ((cells, rays), f32)],
            [column, pltpu.VMEM((rows, features), f32)],
            f"up_{level}",
        )(keep, theirs, depths, depths_in)

    theirs = swap(send, "cell", levels - 1)
    depths_in = swap(depths, "cell", levels - 1)
    color, later, later_send, depths = kernel_call(
        functools.partial(top_body, levels - 1, rays),
        [(keep.shape, bf16), ((8, rays), f32), ((8, rays), f32), ((cells, rays), f32)],
        [column],
        "top",
    )(keep, theirs, depths, depths_in, *held[-1], target_color)

    for level in reversed(range(levels - 2)):
        color_in = swap(color, "cell", level + 1)
        later_in = swap(later_send, "cell", level + 1)
        color, later, later_send = kernel_call(
            functools.partial(down_body, level, rays),
            [((2 * color.shape[0], features), bf16), ((8, rays), f32), ((8, rays), f32)],
            [column],
            f"down_{level}",
        )(color, color_in, later, later_in, depths, *held[level], target_color)

    color_in = swap(color, "cell", 0)
    later_in = swap(later_send, "cell", 0)
    part = (hidden, features // 2)
    whole, grad_depth, pulled, *grads = kernel_call(
        functools.partial(feature_body, rays),
        [((rays, features), bf16), ((8, rays), f32), ((hidden, rays), f32), (part, bf16),
         (part, bf16)],
        (),
        "feature",
    )(color, color_in, later, later_in, depths, target_color, mean_hidden, w_feature_b)
    grads += kernel_call(
        functools.partial(hidden_body, rays), [((hidden, hidden), bf16)], (), "hidden", 12
    )(pulled, grad_depth, hidden_one, hidden_two, logit, step, count, density)

    rendered, depth_grad = kernel_call(
        output_body, [((features // cells, rays), bf16), ((1, rays), f32)], (), "outputs"
    )(whole, grad_depth)

    total = ()
    for turn in range(spread):
        arrived = [swap_groups(grad, turn) for grad in grads]
        for i, (grad, other) in enumerate(zip(grads, arrived)):
            if turn < spread - 1:
                (grads[i],) = kernel_call(add_body, [(grad.shape, bf16)], (), f"add_{i}")(
                    grad, other
                )
            else:
                grads[i], *total = kernel_call(
                    square_body, [(grad.shape, f32), ((8, LANES), f32)], (), f"square_{i}"
                )(grad, other, *total)
    (total,) = total

    for level in range(levels):
        total_in = swap(total, "cell", level)
        if level < levels - 1:
            total = total + total_in

    entries = cells * (hidden * features + hidden * hidden)
    update_second, update_feature = kernel_call(
        functools.partial(adam_body, entries),
        [((hidden, hidden), bf16), ((hidden, features), bf16)],
        (),
        "adam",
    )(total, total_in, *grads, mean_second[0], square_second[0], mean_feature[0],
      square_feature[0])
    return (rendered.T, depth_grad.T, update_second[None], update_feature[None])


def solution(mesh):
    in_specs = (
        P("rays", "cell", None),
        P("rays", "cell"),
        P("rays", "cell"),
        P("rays", "cell"),
        P("cell", None, None),
        P("cell", None, None),
        P("cell", None, None),
        P("cell", None),
        P("cell", None, None),
        P("cell", None, None),
        P("cell", None, None),
        P("cell", None, None),
        P("cell", None, None),
        P("rays", None),
    )
    out_specs = (P("rays", "cell"), P("rays", "cell"), P("cell", None, None), P("cell", None, None))
    return jax.shard_map(
        on_device, mesh=mesh, in_specs=in_specs, out_specs=out_specs, check_vma=False
    )
```

```python
import functools

import jax
import jax.numpy as jnp
from jax import lax
from jax.experimental import pallas as pl
from jax.experimental.pallas import tpu as pltpu
from jax.sharding import PartitionSpec as P


SAMPLES = 8
ADAM_BLOCKS = 4
FEATURE_PARTS = 2
LANES = 128

beta_first = 0.9
beta_second = 0.999
bias_first = 0.19
bias_second = 0.001999
adam_floor = 1e-08
mean_floor = 1e-06

bf16 = jnp.bfloat16
f32 = jnp.float32

NN = (((1,), (0,)), ((), ()))
NT = (((1,), (1,)), ((), ()))


def mm(a, b, dims=NN):
    return lax.dot_general(a, b, dims, preferred_element_type=f32)


def split_high_low(value):
    high = value.astype(bf16)
    return high, (value - high.astype(f32)).astype(bf16)


def kernel_call(body, outs, scratch=(), name=None, limit=8, space=pltpu.VMEM,
                out_space=pltpu.VMEM):
    def call(*args):
        if space is pltpu.HBM:
            args = [pltpu.with_memory_space_constraint(arg, pltpu.HBM) for arg in args]
        return pl.pallas_call(
            body,
            out_shape=tuple(jax.ShapeDtypeStruct(s, d) for s, d in outs),
            in_specs=[pl.BlockSpec(memory_space=space)] * len(args),
            out_specs=tuple(pl.BlockSpec(memory_space=out_space) for _ in outs),
            scratch_shapes=list(scratch),
            compiler_params=pltpu.CompilerParams(vmem_limit_bytes=limit << 20),
            name=name,
        )(*args)

    return call


def bit_of(cell, level):
    return lax.rem(lax.div(cell, 1 << level), 2)


def row_offset(cell, level, rays):
    start = jnp.int32(0)
    for lower in range(level):
        start = start + bit_of(cell, lower) * (rays >> (lower + 1))
    return start


def low_start(cell, level):
    return lax.div(cell, 2 << level) * (2 << level)


def depth_between(depths, first, last):
    place = lax.broadcasted_iota(jnp.int32, depths.shape, 0)
    inside = jnp.logical_and(place >= first, place < last)
    return jnp.sum(jnp.where(inside, depths, 0.0), axis=0, keepdims=True)


def to_column(row):
    return jnp.transpose(jnp.broadcast_to(row, (LANES, row.shape[1])))


def wide(column, width):
    return jnp.concatenate([column] * (width // LANES), axis=1)


def forward_body(
    rays,
    entry_hbm,
    count_hbm,
    step_hbm,
    density_hbm,
    w_first_hbm,
    table_hbm,
    code_hbm,
    w_second_hbm,
    w_feature_hbm,
    keep_ref,
    send_ref,
    depth_ref,
    hidden_one_ref,
    hidden_two_ref,
    mean_hidden_ref,
    w_feature_out_ref,
    logit_ref,
    step_out_ref,
    count_out_ref,
    density_out_ref,
    partial_ref,
    entry_ref,
    w_first_ref,
    table_ref,
    code_ref,
    w_second_ref,
    w_feature_ref,
    done,
):
    cell = lax.axis_index("cell")
    pairs = (
        (w_first_hbm, w_first_ref),
        (table_hbm, table_ref),
        (code_hbm, code_ref),
        (entry_hbm, entry_ref),
        (w_second_hbm, w_second_ref),
        (density_hbm, density_out_ref),
        (count_hbm, count_out_ref),
        (step_hbm, step_out_ref),
        (w_feature_hbm, w_feature_ref),
    )
    copies = [pltpu.make_async_copy(a, b, done.at[i]) for i, (a, b) in enumerate(pairs)]
    for copy in copies:
        copy.start()
    copies[0].wait()
    w_first_t = jnp.transpose(w_first_ref[...].astype(f32)).astype(bf16)
    copies[1].wait()
    rows = table_ref.shape[0]
    table = jnp.concatenate(split_high_low(mm(w_first_t, table_ref[...], NT)), axis=1)
    copies[2].wait()
    code = mm(w_first_t, code_ref[...], NT)
    for copy in copies[3:8]:
        copy.wait()
    w_second_t = jnp.transpose(w_second_ref[...]).astype(bf16)
    density = density_columns(density_out_ref, rays)
    entry = entry_ref[...]
    slot = lax.broadcasted_iota(jnp.int32, (rows, rays), 0)
    for k in range(SAMPLES):
        cols = pl.ds(k * rays, rays)
        hot = (slot == entry + k).astype(f32).astype(bf16)
        hidden_one = jnp.maximum(mm(table, jnp.concatenate([hot, hot], axis=0)) + code, 0.0)
        hidden_one = hidden_one.astype(bf16)
        hidden_one_ref[:, cols] = hidden_one
        hidden_two = jnp.maximum(mm(w_second_t, hidden_one), 0.0).astype(bf16)
        hidden_two_ref[:, cols] = hidden_two
        logit_ref[k : k + 1, :] = jnp.sum(hidden_two.astype(f32) * density, axis=0, keepdims=True)
    depth_steps, weights, _ = slot_scalars(logit_ref[...], step_out_ref[...], count_out_ref[...])
    mean_hidden = jnp.zeros(mean_hidden_ref.shape, f32)
    for k in range(SAMPLES):
        mean_hidden += weights[k] * hidden_two_ref[:, pl.ds(k * rays, rays)].astype(f32)
    mean_hidden_ref[...] = mean_hidden
    copies[8].wait()
    w_feature = w_feature_ref[...].astype(bf16)
    w_feature_out_ref[...] = w_feature
    high, low = split_high_low(jnp.transpose(mean_hidden))
    partial_ref[...] = mm(high, w_feature) + mm(low, w_feature)
    half = keep_ref.shape[0]
    mine = lax.rem(cell, 2)
    keep_ref[...] = partial_ref[pl.ds(pl.multiple_of(mine * half, half), half), :].astype(bf16)
    send_ref[...] = partial_ref[
        pl.ds(pl.multiple_of((1 - mine) * half, half), half), :
    ].astype(bf16)
    place = lax.broadcasted_iota(jnp.int32, depth_ref.shape, 0)
    total = functools.reduce(lambda a, b: a + b, depth_steps)
    depth_ref[...] = jnp.where(place == cell, jnp.broadcast_to(total, depth_ref.shape), 0.0)


def density_columns(density_ref, rays):
    density = density_ref[...].astype(f32)
    return wide(jnp.transpose(jnp.broadcast_to(density, (LANES, density.shape[1]))), rays)


def slot_scalars(logit, step_length, count):
    soft = jnp.maximum(logit, 0.0) + jnp.log1p(jnp.exp(-jnp.abs(logit)))
    depth_steps, weights, behinds = [], [], []
    ahead = jnp.zeros_like(step_length)
    for k in range(SAMPLES):
        travel = jnp.where(k < count, step_length, 0.0)
        depth = soft[k : k + 1, :] * travel
        weights.append(jnp.exp(-ahead) * (1.0 - jnp.exp(-depth)))
        ahead = ahead + depth
        behinds.append(jnp.exp(-ahead))
        depth_steps.append(depth)
    return depth_steps, weights, behinds


def joined(cell, level, rays, mine, theirs, depths, column_ref):
    count = mine.shape[0]
    start = low_start(cell, level)
    fade = jnp.exp(-depth_between(depths, start, start + (1 << level)))
    column_ref[...] = to_column(fade)
    offset = row_offset(cell, level + 1 if count < (rays >> level) else level, rays)
    fade = column_ref[pl.ds(pl.multiple_of(offset, count), count), :]
    is_low = bit_of(cell, level) == 0
    own = wide(jnp.where(is_low, 1.0, fade), mine.shape[1])
    other = wide(jnp.where(is_low, fade, 1.0), mine.shape[1])
    return own * mine.astype(f32) + other * theirs.astype(f32)


def up_body(
    level, rays, mine_ref, theirs_ref, depth_ref, depth_in_ref, keep_ref, send_ref, depth_out_ref,
    column_ref, joined_ref,
):
    cell = lax.axis_index("cell")
    depths = depth_ref[...] + depth_in_ref[...]
    depth_out_ref[...] = depths
    value = joined(cell, level, rays, mine_ref[...], theirs_ref[...], depths, column_ref)
    count, half = value.shape[0], keep_ref.shape[0]
    if half == count:
        keep_ref[...] = value.astype(bf16)
        send_ref[...] = value.astype(bf16)
    else:
        joined_ref[...] = value
        mine = bit_of(cell, level + 1)
        keep_ref[...] = joined_ref[pl.ds(pl.multiple_of(mine * half, half), half), :].astype(bf16)
        send_ref[...] = joined_ref[
            pl.ds(pl.multiple_of((1 - mine) * half, half), half), :
        ].astype(bf16)


def later_light(cell, level, rays, residual, mine, theirs, depths, column_ref):
    count = residual.shape[0]
    high = jnp.where(bit_of(cell, level) == 0, theirs.astype(f32), mine.astype(f32))
    dots = jnp.sum(high * residual, axis=1, keepdims=True)
    offset = row_offset(cell, level if count == (rays >> level) else level + 1, rays)
    column_ref[...] = jnp.zeros_like(column_ref)
    column_ref[pl.ds(pl.multiple_of(offset, count), count), :] = jnp.broadcast_to(
        dots, (count, LANES)
    )
    row = jnp.transpose(column_ref[...])[0:1, :]
    transmit = jnp.exp(-depth_between(depths, 0, low_start(cell, level) + (1 << level)))
    return transmit * row


def share_light(cell, level, later, light, own_ref, their_ref):
    is_low = bit_of(cell, level) == 0
    own_ref[...] = jnp.broadcast_to(later + jnp.where(is_low, light, 0.0), own_ref.shape)
    their_ref[...] = jnp.broadcast_to(later + jnp.where(is_low, 0.0, light), their_ref.shape)


def top_body(
    level, rays, mine_ref, theirs_ref, depth_ref, depth_in_ref, under_mine_ref, under_theirs_ref,
    target_ref, color_ref, later_ref, later_send_ref, depth_out_ref, column_ref,
):
    cell = lax.axis_index("cell")
    depths = depth_ref[...] + depth_in_ref[...]
    depth_out_ref[...] = depths
    mine, theirs = mine_ref[...], theirs_ref[...]
    color = joined(cell, level, rays, mine, theirs, depths, column_ref).astype(bf16)
    color_ref[...] = color
    count = color.shape[0]
    offset = pl.multiple_of(row_offset(cell, level, rays), count)
    residual = color.astype(f32) - target_ref[pl.ds(offset, count), :].astype(f32)
    light = later_light(cell, level, rays, residual, mine, theirs, depths, column_ref)
    later = jnp.where(bit_of(cell, level) == 0, light, 0.0)
    light = later_light(
        cell, level - 1, rays, residual, under_mine_ref[...], under_theirs_ref[...], depths,
        column_ref,
    )
    share_light(cell, level - 1, later, light, later_ref, later_send_ref)


def assembled(cell, level, mine, theirs, out_ref):
    count = mine.shape[0]
    bit = bit_of(cell, level)
    out_ref[pl.ds(pl.multiple_of(bit * count, count), count), :] = mine
    out_ref[pl.ds(pl.multiple_of((1 - bit) * count, count), count), :] = theirs


def down_body(
    level, rays, color_ref, color_in_ref, later_ref, later_in_ref, depth_ref, mine_ref, theirs_ref,
    target_ref, color_out_ref, later_out_ref, later_send_ref, column_ref,
):
    cell = lax.axis_index("cell")
    assembled(cell, level + 1, color_ref[...], color_in_ref[...], color_out_ref)
    later = later_ref[0:1, :] + later_in_ref[0:1, :]
    count = color_out_ref.shape[0]
    offset = pl.multiple_of(row_offset(cell, level + 1, rays), count)
    residual = color_out_ref[...].astype(f32) - target_ref[pl.ds(offset, count), :].astype(f32)
    light = later_light(
        cell, level, rays, residual, mine_ref[...], theirs_ref[...], depth_ref[...], column_ref
    )
    share_light(cell, level, later, light, later_out_ref, later_send_ref)


def feature_body(
    rays,
    color_ref,
    color_in_ref,
    later_ref,
    later_in_ref,
    depth_ref,
    target_ref,
    mean_hidden_ref,
    w_feature_ref,
    whole_ref,
    grad_depth_ref,
    pulled_ref,
    *grad_refs,
):
    cell = lax.axis_index("cell")
    grad_depth_ref[...] = -(later_ref[...] + later_in_ref[...])
    assembled(cell, 0, color_ref[...], color_in_ref[...], whole_ref)
    color = whole_ref[...]
    residual = (color.astype(f32) - target_ref[...].astype(f32)).astype(bf16)
    transmit = jnp.exp(-depth_between(depth_ref[...], 0, cell))
    seen = (mean_hidden_ref[...] * transmit).astype(bf16)
    start = 0
    for ref in grad_refs:
        ref[...] = mm(seen, residual[:, start : start + ref.shape[1]]).astype(bf16)
        start += ref.shape[1]
    pulled_ref[...] = mm(w_feature_ref[...], residual, NT) * transmit


def output_body(color_ref, grad_depth_ref, rendered_ref, depth_grad_ref):
    cell = lax.axis_index("cell")
    width, channels = rendered_ref.shape[0], color_ref.shape[1]
    place = lax.broadcasted_iota(jnp.int32, (width, channels), 0)
    channel = lax.broadcasted_iota(jnp.int32, (width, channels), 1)
    chosen = (channel == place + cell * width).astype(f32).astype(bf16)
    rendered_ref[...] = mm(chosen, color_ref[...], NT).astype(bf16)
    depth_grad_ref[...] = grad_depth_ref[0:1, :]


def hidden_body(
    rays,
    pulled_ref,
    grad_depth_ref,
    hidden_one_ref,
    hidden_two_ref,
    logit_ref,
    step_ref,
    count_ref,
    density_ref,
    second_ref,
):
    hidden = hidden_one_ref.shape[0]
    pulled, grad_depth = pulled_ref[...], grad_depth_ref[0:1, :]
    logit = logit_ref[...]
    _, weights, behinds = slot_scalars(logit, step_ref[...], count_ref[...])
    small = jnp.exp(-jnp.abs(logit))
    sigmoid = jnp.where(logit >= 0.0, 1.0, small) / (1.0 + small)
    dots = [
        jnp.sum(hidden_two_ref[:, pl.ds(k * rays, rays)].astype(f32) * pulled, axis=0, keepdims=True)
        for k in range(SAMPLES)
    ]
    later = jnp.zeros_like(grad_depth)
    grad_logits = [None] * SAMPLES
    for k in reversed(range(SAMPLES)):
        grad_step = behinds[k] * dots[k] - later + grad_depth
        later = later + weights[k] * dots[k]
        travel = jnp.where(k < count_ref[...], step_ref[...], 0.0)
        grad_logits[k] = grad_step * travel * sigmoid[k : k + 1, :]
    density = density_columns(density_ref, rays)
    grad_second = jnp.zeros((hidden, hidden), f32)
    for k in range(SAMPLES):
        cols = pl.ds(k * rays, rays)
        grad_hidden = weights[k] * pulled + grad_logits[k] * density
        grad_before = jnp.where(hidden_two_ref[:, cols].astype(f32) > 0, grad_hidden, 0.0)
        grad_second += mm(hidden_one_ref[:, cols], grad_before.astype(bf16), NT)
    second_ref[...] = grad_second.astype(bf16)


def add_body(a_ref, b_ref, out_ref):
    out_ref[...] = (a_ref[...].astype(f32) + b_ref[...].astype(f32)).astype(out_ref.dtype)


def square_body(a_ref, b_ref, *rest):
    *before_ref, out_ref, sum_ref = rest
    value = a_ref[...].astype(f32) + b_ref[...].astype(f32)
    out_ref[...] = value
    total = jnp.sum(jnp.sum(value * value, axis=0, keepdims=True), axis=1, keepdims=True)
    total = jnp.broadcast_to(total, sum_ref.shape)
    sum_ref[...] = total + before_ref[0][...] if before_ref else total


def adam_of(gradient, mean_moment, square_moment, rescale):
    unit_grad = gradient * rescale
    mean_new = (beta_first / bias_first) * mean_moment + ((1.0 - beta_first) / bias_first) * unit_grad
    square_new = (beta_second / bias_second) * square_moment + (
        (1.0 - beta_second) / bias_second
    ) * (unit_grad * unit_grad)
    return (mean_new / (square_new * lax.rsqrt(square_new) + adam_floor)).astype(bf16)


def adam_body(entries, sum_ref, sum_in_ref, *rest):
    *in_refs, update_second_hbm, update_feature_hbm, second_ref, feature_ref, done = rest
    *grad_refs, mean_second_ref, square_second_ref, mean_feature_ref, square_feature_ref = in_refs
    *part_refs, last_ref = grad_refs
    rescale = lax.rsqrt((sum_ref[0:1, :] + sum_in_ref[0:1, :]) / entries + mean_floor)
    block = feature_ref.shape[0] // ADAM_BLOCKS
    copies = []
    for i in range(ADAM_BLOCKS):
        rows = pl.ds(i * block, block)
        start = 0
        for ref in part_refs:
            cols = pl.ds(start, ref.shape[1])
            feature_ref[rows, cols] = adam_of(
                ref[rows, :], mean_feature_ref[rows, cols], square_feature_ref[rows, cols],
                wide(rescale, ref.shape[1]),
            )
            start += ref.shape[1]
        second_ref[rows, :] = adam_of(
            last_ref[rows, :], mean_second_ref[rows, :], square_second_ref[rows, :],
            wide(rescale, second_ref.shape[1]),
        )
        for j, (value, out) in enumerate(
            ((feature_ref, update_feature_hbm), (second_ref, update_second_hbm))
        ):
            copy = pltpu.make_async_copy(value.at[rows], out.at[rows], done.at[i, j])
            copy.start()
            copies.append(copy)
    for copy in copies:
        copy.wait()


def swap(value, axis, bit):
    count = lax.axis_size(axis)
    return lax.ppermute(value, axis, [(i, i ^ (1 << bit)) for i in range(count)])


def swap_crossed(value, level):
    count = lax.axis_size("cell")
    flip = 1 << level | 1
    return lax.ppermute(value, "cell", [(i, i ^ flip) for i in range(count)])


def swap_groups(value, turn):
    cells, groups = lax.axis_size("cell"), lax.axis_size("rays")
    spread = groups.bit_length() - 1
    pairs = [
        (c * groups + g, c * groups + (g ^ (1 << ((turn + c) % spread))))
        for c in range(cells)
        for g in range(groups)
    ]
    return lax.ppermute(value, ("cell", "rays"), pairs)


def on_device(
    ray_code,
    entry_index,
    sample_count,
    step_length,
    positions,
    w_first,
    w_second,
    w_density,
    w_feature,
    mean_second,
    square_second,
    mean_feature,
    square_feature,
    target_color,
):
    rays, _, hidden = ray_code.shape
    features = w_feature.shape[2]
    cells = lax.axis_size("cell")
    groups = lax.axis_size("rays")
    levels = cells.bit_length() - 1
    spread = groups.bit_length() - 1
    entry, count, step = entry_index.T, sample_count.T, step_length.T
    column = pltpu.VMEM((rays, LANES), f32)

    half = rays // 2
    (
        keep, send, depths, hidden_one, hidden_two, mean_hidden, w_feature_b, logit, step, count,
        density,
    ) = kernel_call(
        functools.partial(forward_body, rays),
        [
            ((half, features), bf16),
            ((half, features), bf16),
            ((cells, rays), f32),
            ((hidden, SAMPLES * rays), bf16),
            ((hidden, SAMPLES * rays), bf16),
            ((hidden, rays), f32),
            ((hidden, features), bf16),
            ((SAMPLES, rays), f32),
            (step.shape, f32),
            (count.shape, jnp.int32),
            (w_density.shape, bf16),
        ],
        [
            pltpu.VMEM((rays, features), f32),
            pltpu.VMEM(entry.shape, jnp.int32),
            pltpu.VMEM(w_first.shape[1:], bf16),
            pltpu.VMEM(positions.shape[1:], bf16),
            pltpu.VMEM((rays, hidden), bf16),
            pltpu.VMEM(w_second.shape[1:], f32),
            pltpu.VMEM(w_feature.shape[1:], f32),
            pltpu.SemaphoreType.DMA((9,)),
        ],
        "forward",
        16,
        pltpu.HBM,
    )(entry, count, step, w_density, w_first[0], positions[0], ray_code[:, 0, :], w_second[0],
      w_feature[0])

    held = []
    for level in range(levels - 1):
        theirs = swap(send, "cell", level)
        depths_in = swap(depths, "cell", level)
        held.append((keep, theirs))
        rows = keep.shape[0]
        next_rows = rows if level == levels - 2 else rows // 2
        keep, send, depths = kernel_call(
            functools.partial(up_body, level, rays),
            [((next_rows, features), bf16), ((next_rows, features), bf16), ((cells, rays), f32)],
            [column, pltpu.VMEM((rows, features), f32)],
            f"up_{level}",
        )(keep, theirs, depths, depths_in)

    theirs = swap(send, "cell", levels - 1)
    depths_in = swap(depths, "cell", levels - 1)
    color, later, later_send, depths = kernel_call(
        functools.partial(top_body, levels - 1, rays),
        [(keep.shape, bf16), ((8, rays), f32), ((8, rays), f32), ((cells, rays), f32)],
        [column],
        "top",
    )(keep, theirs, depths, depths_in, *held[-1], target_color)

    for level in reversed(range(levels - 2)):
        color_in = swap(color, "cell", level + 1)
        later_in = swap(later_send, "cell", level + 1)
        color, later, later_send = kernel_call(
            functools.partial(down_body, level, rays),
            [((2 * color.shape[0], features), bf16), ((8, rays), f32), ((8, rays), f32)],
            [column],
            f"down_{level}",
        )(color, color_in, later, later_in, depths, *held[level], target_color)

    color_in = swap(color, "cell", 0)
    later_in = swap(later_send, "cell", 0)
    part = (hidden, features // FEATURE_PARTS)
    whole, grad_depth, pulled, *grads = kernel_call(
        functools.partial(feature_body, rays),
        [((rays, features), bf16), ((8, rays), f32), ((hidden, rays), f32)]
        + [(part, bf16)] * FEATURE_PARTS,
        (),
        "feature",
    )(color, color_in, later, later_in, depths, target_color, mean_hidden, w_feature_b)
    grads += kernel_call(
        functools.partial(hidden_body, rays), [((hidden, hidden), bf16)], (), "hidden", 12
    )(pulled, grad_depth, hidden_one, hidden_two, logit, step, count, density)
    rendered, depth_grad = kernel_call(
        output_body, [((features // cells, rays), bf16), ((1, rays), f32)], (), "outputs"
    )(whole, grad_depth)

    total = ()
    for turn in range(spread):
        arrived = [swap_groups(grad, turn) for grad in grads]
        for i, (grad, other) in enumerate(zip(grads, arrived)):
            if turn < spread - 1:
                (grads[i],) = kernel_call(add_body, [(grad.shape, bf16)], (), f"add_{i}")(
                    grad, other
                )
            else:
                grads[i], *total = kernel_call(
                    square_body, [(grad.shape, f32), ((8, LANES), f32)], (), f"square_{i}"
                )(grad, other, *total)
    (total,) = total

    for level in range(levels):
        total_in = swap_crossed(total, level)
        if level < levels - 1:
            total = total + total_in

    entries = cells * (hidden * features + hidden * hidden)
    update_second, update_feature = kernel_call(
        functools.partial(adam_body, entries),
        [((hidden, hidden), bf16), ((hidden, features), bf16)],
        [
            pltpu.VMEM((hidden, hidden), bf16),
            pltpu.VMEM((hidden, features), bf16),
            pltpu.SemaphoreType.DMA((ADAM_BLOCKS, 2)),
        ],
        "adam",
        out_space=pltpu.HBM,
    )(total, total_in, *grads, mean_second[0], square_second[0], mean_feature[0],
      square_feature[0])
    return (rendered.T, depth_grad.T, update_second[None], update_feature[None])


def solution(mesh):
    in_specs = (
        P("rays", "cell", None),
        P("rays", "cell"),
        P("rays", "cell"),
        P("rays", "cell"),
        P("cell", None, None),
        P("cell", None, None),
        P("cell", None, None),
        P("cell", None),
        P("cell", None, None),
        P("cell", None, None),
        P("cell", None, None),
        P("cell", None, None),
        P("cell", None, None),
        P("rays", None),
    )
    out_specs = (P("rays", "cell"), P("rays", "cell"), P("cell", None, None), P("cell", None, None))
    return jax.shard_map(
        on_device, mesh=mesh, in_specs=in_specs, out_specs=out_specs, check_vma=False
    )
```

```python
import functools

import jax
import jax.numpy as jnp
from jax import lax
from jax.experimental import pallas as pl
from jax.experimental.pallas import tpu as pltpu
from jax.sharding import PartitionSpec as P


SAMPLES = 8
ADAM_BLOCKS = 4
FEATURE_PARTS = 2
LANES = 128

beta_first = 0.9
beta_second = 0.999
bias_first = 0.19
bias_second = 0.001999
adam_floor = 1e-08
mean_floor = 1e-06

bf16 = jnp.bfloat16
f32 = jnp.float32

NN = (((1,), (0,)), ((), ()))
NT = (((1,), (1,)), ((), ()))


def mm(a, b, dims=NN):
    return lax.dot_general(a, b, dims, preferred_element_type=f32)


def split_high_low(value):
    high = value.astype(bf16)
    return high, (value - high.astype(f32)).astype(bf16)


def kernel_call(body, outs, scratch=(), name=None, limit=8, space=pltpu.VMEM,
                out_space=pltpu.VMEM):
    def call(*args):
        if space is pltpu.HBM:
            args = [pltpu.with_memory_space_constraint(arg, pltpu.HBM) for arg in args]
        return pl.pallas_call(
            body,
            out_shape=tuple(jax.ShapeDtypeStruct(s, d) for s, d in outs),
            in_specs=[pl.BlockSpec(memory_space=space)] * len(args),
            out_specs=tuple(pl.BlockSpec(memory_space=out_space) for _ in outs),
            scratch_shapes=list(scratch),
            compiler_params=pltpu.CompilerParams(vmem_limit_bytes=limit << 20),
            name=name,
        )(*args)

    return call


def bit_of(cell, level):
    return lax.rem(lax.div(cell, 1 << level), 2)


def row_offset(cell, level, rays):
    start = jnp.int32(0)
    for lower in range(level):
        start = start + bit_of(cell, lower) * (rays >> (lower + 1))
    return start


def low_start(cell, level):
    return lax.div(cell, 2 << level) * (2 << level)


def depth_between(depths, first, last):
    place = lax.broadcasted_iota(jnp.int32, depths.shape, 0)
    inside = jnp.logical_and(place >= first, place < last)
    return jnp.sum(jnp.where(inside, depths, 0.0), axis=0, keepdims=True)


def to_column(row):
    return jnp.transpose(jnp.broadcast_to(row, (LANES, row.shape[1])))


def wide(column, width):
    return jnp.concatenate([column] * (width // LANES), axis=1)


def forward_body(
    rays,
    entry_hbm,
    count_hbm,
    step_hbm,
    density_hbm,
    w_first_hbm,
    table_hbm,
    code_hbm,
    w_second_hbm,
    w_feature_hbm,
    keep_ref,
    send_ref,
    depth_ref,
    hidden_one_ref,
    hidden_two_ref,
    mean_hidden_ref,
    w_feature_out_ref,
    logit_ref,
    step_out_ref,
    count_out_ref,
    density_out_ref,
    partial_ref,
    entry_ref,
    w_first_ref,
    table_ref,
    code_ref,
    w_second_ref,
    w_feature_ref,
    done,
):
    cell = lax.axis_index("cell")
    pairs = (
        (w_first_hbm, w_first_ref),
        (table_hbm, table_ref),
        (code_hbm, code_ref),
        (entry_hbm, entry_ref),
        (w_second_hbm, w_second_ref),
        (density_hbm, density_out_ref),
        (count_hbm, count_out_ref),
        (step_hbm, step_out_ref),
        (w_feature_hbm, w_feature_ref),
    )
    copies = [pltpu.make_async_copy(a, b, done.at[i]) for i, (a, b) in enumerate(pairs)]
    for copy in copies:
        copy.start()
    copies[0].wait()
    w_first_t = jnp.transpose(w_first_ref[...].astype(f32)).astype(bf16)
    copies[1].wait()
    rows = table_ref.shape[0]
    table = jnp.concatenate(split_high_low(mm(w_first_t, table_ref[...], NT)), axis=1)
    copies[2].wait()
    code = mm(w_first_t, code_ref[...], NT)
    for copy in copies[3:8]:
        copy.wait()
    w_second_t = jnp.transpose(w_second_ref[...]).astype(bf16)
    density = density_columns(density_out_ref, rays)
    entry = entry_ref[...]
    slot = lax.broadcasted_iota(jnp.int32, (rows, rays), 0)
    for k in range(SAMPLES):
        cols = pl.ds(k * rays, rays)
        hot = (slot == entry + k).astype(f32).astype(bf16)
        hidden_one = jnp.maximum(mm(table, jnp.concatenate([hot, hot], axis=0)) + code, 0.0)
        hidden_one = hidden_one.astype(bf16)
        hidden_one_ref[:, cols] = hidden_one
        hidden_two = jnp.maximum(mm(w_second_t, hidden_one), 0.0).astype(bf16)
        hidden_two_ref[:, cols] = hidden_two
        logit_ref[k : k + 1, :] = jnp.sum(hidden_two.astype(f32) * density, axis=0, keepdims=True)
    depth_steps, weights, _ = slot_scalars(logit_ref[...], step_out_ref[...], count_out_ref[...])
    mean_hidden = jnp.zeros(mean_hidden_ref.shape, f32)
    for k in range(SAMPLES):
        mean_hidden += weights[k] * hidden_two_ref[:, pl.ds(k * rays, rays)].astype(f32)
    mean_hidden_ref[...] = mean_hidden
    copies[8].wait()
    w_feature = w_feature_ref[...].astype(bf16)
    w_feature_out_ref[...] = w_feature
    high, low = split_high_low(jnp.transpose(mean_hidden))
    partial_ref[...] = mm(high, w_feature) + mm(low, w_feature)
    half = keep_ref.shape[0]
    mine = lax.rem(cell, 2)
    keep_ref[...] = partial_ref[pl.ds(pl.multiple_of(mine * half, half), half), :].astype(bf16)
    send_ref[...] = partial_ref[
        pl.ds(pl.multiple_of((1 - mine) * half, half), half), :
    ].astype(bf16)
    place = lax.broadcasted_iota(jnp.int32, depth_ref.shape, 0)
    total = functools.reduce(lambda a, b: a + b, depth_steps)
    depth_ref[...] = jnp.where(place == cell, jnp.broadcast_to(total, depth_ref.shape), 0.0)


def density_columns(density_ref, rays):
    density = density_ref[...].astype(f32)
    return wide(jnp.transpose(jnp.broadcast_to(density, (LANES, density.shape[1]))), rays)


def slot_scalars(logit, step_length, count):
    soft = jnp.maximum(logit, 0.0) + jnp.log1p(jnp.exp(-jnp.abs(logit)))
    depth_steps, weights, behinds = [], [], []
    ahead = jnp.zeros_like(step_length)
    for k in range(SAMPLES):
        travel = jnp.where(k < count, step_length, 0.0)
        depth = soft[k : k + 1, :] * travel
        weights.append(jnp.exp(-ahead) * (1.0 - jnp.exp(-depth)))
        ahead = ahead + depth
        behinds.append(jnp.exp(-ahead))
        depth_steps.append(depth)
    return depth_steps, weights, behinds


def joined(cell, level, rays, mine, theirs, depths, column_ref):
    count = mine.shape[0]
    start = low_start(cell, level)
    fade = jnp.exp(-depth_between(depths, start, start + (1 << level)))
    column_ref[...] = to_column(fade)
    offset = row_offset(cell, level + 1 if count < (rays >> level) else level, rays)
    fade = column_ref[pl.ds(pl.multiple_of(offset, count), count), :]
    is_low = bit_of(cell, level) == 0
    own = wide(jnp.where(is_low, 1.0, fade), mine.shape[1])
    other = wide(jnp.where(is_low, fade, 1.0), mine.shape[1])
    return own * mine.astype(f32) + other * theirs.astype(f32)


def up_body(
    level, rays, mine_ref, theirs_ref, depth_ref, depth_in_ref, keep_ref, send_ref, depth_out_ref,
    column_ref, joined_ref,
):
    cell = lax.axis_index("cell")
    depths = depth_ref[...] + depth_in_ref[...]
    depth_out_ref[...] = depths
    value = joined(cell, level, rays, mine_ref[...], theirs_ref[...], depths, column_ref)
    count, half = value.shape[0], keep_ref.shape[0]
    if half == count:
        keep_ref[...] = value.astype(bf16)
        send_ref[...] = value.astype(bf16)
    else:
        joined_ref[...] = value
        mine = bit_of(cell, level + 1)
        keep_ref[...] = joined_ref[pl.ds(pl.multiple_of(mine * half, half), half), :].astype(bf16)
        send_ref[...] = joined_ref[
            pl.ds(pl.multiple_of((1 - mine) * half, half), half), :
        ].astype(bf16)


def later_light(cell, level, rays, residual, mine, theirs, depths, column_ref):
    count = residual.shape[0]
    high = jnp.where(bit_of(cell, level) == 0, theirs.astype(f32), mine.astype(f32))
    dots = jnp.sum(high * residual, axis=1, keepdims=True)
    offset = row_offset(cell, level if count == (rays >> level) else level + 1, rays)
    column_ref[...] = jnp.zeros_like(column_ref)
    column_ref[pl.ds(pl.multiple_of(offset, count), count), :] = jnp.broadcast_to(
        dots, (count, LANES)
    )
    row = jnp.transpose(column_ref[...])[0:1, :]
    transmit = jnp.exp(-depth_between(depths, 0, low_start(cell, level) + (1 << level)))
    return transmit * row


def share_light(cell, level, later, light, own_ref, their_ref):
    is_low = bit_of(cell, level) == 0
    own_ref[...] = jnp.broadcast_to(later + jnp.where(is_low, light, 0.0), own_ref.shape)
    their_ref[...] = jnp.broadcast_to(later + jnp.where(is_low, 0.0, light), their_ref.shape)


def top_body(
    level, rays, mine_ref, theirs_ref, depth_ref, depth_in_ref, under_mine_ref, under_theirs_ref,
    target_ref, color_ref, later_ref, later_send_ref, depth_out_ref, column_ref,
):
    cell = lax.axis_index("cell")
    depths = depth_ref[...] + depth_in_ref[...]
    depth_out_ref[...] = depths
    mine, theirs = mine_ref[...], theirs_ref[...]
    color = joined(cell, level, rays, mine, theirs, depths, column_ref).astype(bf16)
    color_ref[...] = color
    count = color.shape[0]
    offset = pl.multiple_of(row_offset(cell, level, rays), count)
    residual = color.astype(f32) - target_ref[pl.ds(offset, count), :].astype(f32)
    light = later_light(cell, level, rays, residual, mine, theirs, depths, column_ref)
    later = jnp.where(bit_of(cell, level) == 0, light, 0.0)
    light = later_light(
        cell, level - 1, rays, residual, under_mine_ref[...], under_theirs_ref[...], depths,
        column_ref,
    )
    share_light(cell, level - 1, later, light, later_ref, later_send_ref)


def assembled(cell, level, mine, theirs, out_ref):
    count = mine.shape[0]
    bit = bit_of(cell, level)
    out_ref[pl.ds(pl.multiple_of(bit * count, count), count), :] = mine
    out_ref[pl.ds(pl.multiple_of((1 - bit) * count, count), count), :] = theirs


def down_body(
    level, rays, color_ref, color_in_ref, later_ref, later_in_ref, depth_ref, mine_ref, theirs_ref,
    target_ref, color_out_ref, later_out_ref, later_send_ref, column_ref,
):
    cell = lax.axis_index("cell")
    assembled(cell, level + 1, color_ref[...], color_in_ref[...], color_out_ref)
    later = later_ref[0:1, :] + later_in_ref[0:1, :]
    count = color_out_ref.shape[0]
    offset = pl.multiple_of(row_offset(cell, level + 1, rays), count)
    residual = color_out_ref[...].astype(f32) - target_ref[pl.ds(offset, count), :].astype(f32)
    light = later_light(
        cell, level, rays, residual, mine_ref[...], theirs_ref[...], depth_ref[...], column_ref
    )
    share_light(cell, level, later, light, later_out_ref, later_send_ref)


def feature_body(
    rays,
    color_ref,
    color_in_ref,
    later_ref,
    later_in_ref,
    depth_ref,
    target_ref,
    mean_hidden_ref,
    w_feature_ref,
    whole_ref,
    grad_depth_ref,
    pulled_ref,
    *grad_refs,
):
    cell = lax.axis_index("cell")
    grad_depth_ref[...] = -(later_ref[...] + later_in_ref[...])
    assembled(cell, 0, color_ref[...], color_in_ref[...], whole_ref)
    color = whole_ref[...]
    residual = (color.astype(f32) - target_ref[...].astype(f32)).astype(bf16)
    transmit = jnp.exp(-depth_between(depth_ref[...], 0, cell))
    seen = (mean_hidden_ref[...] * transmit).astype(bf16)
    start = 0
    for ref in grad_refs:
        ref[...] = mm(seen, residual[:, start : start + ref.shape[1]]).astype(bf16)
        start += ref.shape[1]
    pulled_ref[...] = mm(w_feature_ref[...], residual, NT) * transmit


def output_body(color_ref, grad_depth_ref, rendered_ref, depth_grad_ref):
    cell = lax.axis_index("cell")
    width, channels = rendered_ref.shape[0], color_ref.shape[1]
    place = lax.broadcasted_iota(jnp.int32, (width, channels), 0)
    channel = lax.broadcasted_iota(jnp.int32, (width, channels), 1)
    chosen = (channel == place + cell * width).astype(f32).astype(bf16)
    rendered_ref[...] = mm(chosen, color_ref[...], NT).astype(bf16)
    depth_grad_ref[...] = grad_depth_ref[0:1, :]


def hidden_body(
    rays,
    pulled_ref,
    grad_depth_ref,
    hidden_one_ref,
    hidden_two_ref,
    logit_ref,
    step_ref,
    count_ref,
    density_ref,
    second_ref,
):
    hidden = hidden_one_ref.shape[0]
    pulled, grad_depth = pulled_ref[...], grad_depth_ref[0:1, :]
    logit = logit_ref[...]
    _, weights, behinds = slot_scalars(logit, step_ref[...], count_ref[...])
    small = jnp.exp(-jnp.abs(logit))
    sigmoid = jnp.where(logit >= 0.0, 1.0, small) / (1.0 + small)
    dots = [
        jnp.sum(hidden_two_ref[:, pl.ds(k * rays, rays)].astype(f32) * pulled, axis=0, keepdims=True)
        for k in range(SAMPLES)
    ]
    later = jnp.zeros_like(grad_depth)
    grad_logits = [None] * SAMPLES
    for k in reversed(range(SAMPLES)):
        grad_step = behinds[k] * dots[k] - later + grad_depth
        later = later + weights[k] * dots[k]
        travel = jnp.where(k < count_ref[...], step_ref[...], 0.0)
        grad_logits[k] = grad_step * travel * sigmoid[k : k + 1, :]
    density = density_columns(density_ref, rays)
    grad_second = jnp.zeros((hidden, hidden), f32)
    for k in range(SAMPLES):
        cols = pl.ds(k * rays, rays)
        grad_hidden = weights[k] * pulled + grad_logits[k] * density
        grad_before = jnp.where(hidden_two_ref[:, cols].astype(f32) > 0, grad_hidden, 0.0)
        grad_second += mm(hidden_one_ref[:, cols], grad_before.astype(bf16), NT)
    second_ref[...] = grad_second.astype(bf16)


def add_body(a_ref, b_ref, out_ref):
    out_ref[...] = (a_ref[...].astype(f32) + b_ref[...].astype(f32)).astype(out_ref.dtype)


def square_body(a_ref, b_ref, *rest):
    *before_ref, out_ref, sum_ref = rest
    value = a_ref[...].astype(f32) + b_ref[...].astype(f32)
    out_ref[...] = value
    total = jnp.sum(jnp.sum(value * value, axis=0, keepdims=True), axis=1, keepdims=True)
    total = jnp.broadcast_to(total, sum_ref.shape)
    sum_ref[...] = total + before_ref[0][...] if before_ref else total


def adam_of(gradient, mean_moment, square_moment, rescale):
    unit_grad = gradient * rescale
    mean_new = (beta_first / bias_first) * mean_moment + ((1.0 - beta_first) / bias_first) * unit_grad
    square_new = (beta_second / bias_second) * square_moment + (
        (1.0 - beta_second) / bias_second
    ) * (unit_grad * unit_grad)
    return (mean_new / (square_new * lax.rsqrt(square_new) + adam_floor)).astype(bf16)


def adam_body(entries, sum_ref, sum_in_ref, *rest):
    *in_refs, update_second_hbm, update_feature_hbm, second_ref, feature_ref, done = rest
    *grad_refs, mean_second_ref, square_second_ref, mean_feature_ref, square_feature_ref = in_refs
    *part_refs, last_ref = grad_refs
    rescale = lax.rsqrt((sum_ref[0:1, :] + sum_in_ref[0:1, :]) / entries + mean_floor)
    block = feature_ref.shape[0] // ADAM_BLOCKS
    copies = []
    for i in range(ADAM_BLOCKS):
        rows = pl.ds(i * block, block)
        start = 0
        for ref in part_refs:
            cols = pl.ds(start, ref.shape[1])
            feature_ref[rows, cols] = adam_of(
                ref[rows, :], mean_feature_ref[rows, cols], square_feature_ref[rows, cols],
                wide(rescale, ref.shape[1]),
            )
            start += ref.shape[1]
        second_ref[rows, :] = adam_of(
            last_ref[rows, :], mean_second_ref[rows, :], square_second_ref[rows, :],
            wide(rescale, second_ref.shape[1]),
        )
        for j, (value, out) in enumerate(
            ((feature_ref, update_feature_hbm), (second_ref, update_second_hbm))
        ):
            copy = pltpu.make_async_copy(value.at[rows], out.at[rows], done.at[i, j])
            copy.start()
            copies.append(copy)
    for copy in copies:
        copy.wait()


def swap(value, axis, bit):
    count = lax.axis_size(axis)
    return lax.ppermute(value, axis, [(i, i ^ (1 << bit)) for i in range(count)])


def swap_cells(value, flip):
    count = lax.axis_size("cell")
    return lax.ppermute(value, "cell", [(i, i ^ flip) for i in range(count)])


def swap_groups(value, turn):
    cells, groups = lax.axis_size("cell"), lax.axis_size("rays")
    spread = groups.bit_length() - 1
    pairs = [
        (c * groups + g, c * groups + (g ^ (1 << ((turn + c) % spread))))
        for c in range(cells)
        for g in range(groups)
    ]
    return lax.ppermute(value, ("cell", "rays"), pairs)


def on_device(
    ray_code,
    entry_index,
    sample_count,
    step_length,
    positions,
    w_first,
    w_second,
    w_density,
    w_feature,
    mean_second,
    square_second,
    mean_feature,
    square_feature,
    target_color,
):
    rays, _, hidden = ray_code.shape
    features = w_feature.shape[2]
    cells = lax.axis_size("cell")
    groups = lax.axis_size("rays")
    levels = cells.bit_length() - 1
    spread = groups.bit_length() - 1
    entry, count, step = entry_index.T, sample_count.T, step_length.T
    column = pltpu.VMEM((rays, LANES), f32)

    half = rays // 2
    (
        keep, send, depths, hidden_one, hidden_two, mean_hidden, w_feature_b, logit, step, count,
        density,
    ) = kernel_call(
        functools.partial(forward_body, rays),
        [
            ((half, features), bf16),
            ((half, features), bf16),
            ((cells, rays), f32),
            ((hidden, SAMPLES * rays), bf16),
            ((hidden, SAMPLES * rays), bf16),
            ((hidden, rays), f32),
            ((hidden, features), bf16),
            ((SAMPLES, rays), f32),
            (step.shape, f32),
            (count.shape, jnp.int32),
            (w_density.shape, bf16),
        ],
        [
            pltpu.VMEM((rays, features), f32),
            pltpu.VMEM(entry.shape, jnp.int32),
            pltpu.VMEM(w_first.shape[1:], bf16),
            pltpu.VMEM(positions.shape[1:], bf16),
            pltpu.VMEM((rays, hidden), bf16),
            pltpu.VMEM(w_second.shape[1:], f32),
            pltpu.VMEM(w_feature.shape[1:], f32),
            pltpu.SemaphoreType.DMA((9,)),
        ],
        "forward",
        16,
        pltpu.HBM,
    )(entry, count, step, w_density, w_first[0], positions[0], ray_code[:, 0, :], w_second[0],
      w_feature[0])

    held = []
    for level in range(levels - 1):
        theirs = swap(send, "cell", level)
        depths_in = swap(depths, "cell", level)
        held.append((keep, theirs))
        rows = keep.shape[0]
        next_rows = rows if level == levels - 2 else rows // 2
        keep, send, depths = kernel_call(
            functools.partial(up_body, level, rays),
            [((next_rows, features), bf16), ((next_rows, features), bf16), ((cells, rays), f32)],
            [column, pltpu.VMEM((rows, features), f32)],
            f"up_{level}",
        )(keep, theirs, depths, depths_in)

    theirs = swap(send, "cell", levels - 1)
    depths_in = swap(depths, "cell", levels - 1)
    color, later, later_send, depths = kernel_call(
        functools.partial(top_body, levels - 1, rays),
        [(keep.shape, bf16), ((8, rays), f32), ((8, rays), f32), ((cells, rays), f32)],
        [column],
        "top",
    )(keep, theirs, depths, depths_in, *held[-1], target_color)

    for level in reversed(range(levels - 2)):
        color_in = swap(color, "cell", level + 1)
        later_in = swap(later_send, "cell", level + 1)
        color, later, later_send = kernel_call(
            functools.partial(down_body, level, rays),
            [((2 * color.shape[0], features), bf16), ((8, rays), f32), ((8, rays), f32)],
            [column],
            f"down_{level}",
        )(color, color_in, later, later_in, depths, *held[level], target_color)

    color_in = swap(color, "cell", 0)
    later_in = swap(later_send, "cell", 0)
    part = (hidden, features // FEATURE_PARTS)
    whole, grad_depth, pulled, *grads = kernel_call(
        functools.partial(feature_body, rays),
        [((rays, features), bf16), ((8, rays), f32), ((hidden, rays), f32)]
        + [(part, bf16)] * FEATURE_PARTS,
        (),
        "feature",
    )(color, color_in, later, later_in, depths, target_color, mean_hidden, w_feature_b)
    grads += kernel_call(
        functools.partial(hidden_body, rays), [((hidden, hidden), bf16)], (), "hidden", 12
    )(pulled, grad_depth, hidden_one, hidden_two, logit, step, count, density)
    rendered, depth_grad = kernel_call(
        output_body, [((features // cells, rays), bf16), ((1, rays), f32)], (), "outputs"
    )(whole, grad_depth)

    total = ()
    for turn in range(spread):
        arrived = [swap_groups(grad, turn) for grad in grads]
        for i, (grad, other) in enumerate(zip(grads, arrived)):
            if turn < spread - 1:
                (grads[i],) = kernel_call(add_body, [(grad.shape, bf16)], (), f"add_{i}")(
                    grad, other
                )
            else:
                grads[i], *total = kernel_call(
                    square_body, [(grad.shape, f32), ((8, LANES), f32)], (), f"square_{i}"
                )(grad, other, *total)
    (total,) = total

    beside, above, across = (swap_cells(total, flip) for flip in (1, 2, 3))
    total = (total + beside) + (above + across)
    for level in range(2, levels):
        total_in = swap_cells(total, 1 << level | 1)
        if level < levels - 1:
            total = total + total_in

    entries = cells * (hidden * features + hidden * hidden)
    update_second, update_feature = kernel_call(
        functools.partial(adam_body, entries),
        [((hidden, hidden), bf16), ((hidden, features), bf16)],
        [
            pltpu.VMEM((hidden, hidden), bf16),
            pltpu.VMEM((hidden, features), bf16),
            pltpu.SemaphoreType.DMA((ADAM_BLOCKS, 2)),
        ],
        "adam",
        out_space=pltpu.HBM,
    )(total, total_in, *grads, mean_second[0], square_second[0], mean_feature[0],
      square_feature[0])
    return (rendered.T, depth_grad.T, update_second[None], update_feature[None])


def solution(mesh):
    in_specs = (
        P("rays", "cell", None),
        P("rays", "cell"),
        P("rays", "cell"),
        P("rays", "cell"),
        P("cell", None, None),
        P("cell", None, None),
        P("cell", None, None),
        P("cell", None),
        P("cell", None, None),
        P("cell", None, None),
        P("cell", None, None),
        P("cell", None, None),
        P("cell", None, None),
        P("rays", None),
    )
    out_specs = (P("rays", "cell"), P("rays", "cell"), P("cell", None, None), P("cell", None, None))
    return jax.shard_map(
        on_device, mesh=mesh, in_specs=in_specs, out_specs=out_specs, check_vma=False
    )
```

```python
import functools

import jax
import jax.numpy as jnp
from jax import lax
from jax.experimental import pallas as pl
from jax.experimental.pallas import tpu as pltpu
from jax.sharding import PartitionSpec as P


SAMPLES = 8
ADAM_BLOCKS = 4
FEATURE_PARTS = 2
LANES = 128

beta_first = 0.9
beta_second = 0.999
bias_first = 0.19
bias_second = 0.001999
adam_floor = 1e-08
mean_floor = 1e-06

bf16 = jnp.bfloat16
f32 = jnp.float32

NN = (((1,), (0,)), ((), ()))
NT = (((1,), (1,)), ((), ()))


def mm(a, b, dims=NN):
    return lax.dot_general(a, b, dims, preferred_element_type=f32)


def split_high_low(value):
    high = value.astype(bf16)
    return high, (value - high.astype(f32)).astype(bf16)


def kernel_call(body, outs, scratch=(), name=None, limit=8, space=pltpu.VMEM,
                out_space=pltpu.VMEM):
    def call(*args):
        if space is pltpu.HBM:
            args = [pltpu.with_memory_space_constraint(arg, pltpu.HBM) for arg in args]
        return pl.pallas_call(
            body,
            out_shape=tuple(jax.ShapeDtypeStruct(s, d) for s, d in outs),
            in_specs=[pl.BlockSpec(memory_space=space)] * len(args),
            out_specs=tuple(pl.BlockSpec(memory_space=out_space) for _ in outs),
            scratch_shapes=list(scratch),
            compiler_params=pltpu.CompilerParams(vmem_limit_bytes=limit << 20),
            name=name,
        )(*args)

    return call


def bit_of(cell, level):
    return lax.rem(lax.div(cell, 1 << level), 2)


def row_offset(cell, level, rays):
    start = jnp.int32(0)
    for lower in range(level):
        start = start + bit_of(cell, lower) * (rays >> (lower + 1))
    return start


def low_start(cell, level):
    return lax.div(cell, 2 << level) * (2 << level)


def depth_between(depths, first, last):
    place = lax.broadcasted_iota(jnp.int32, depths.shape, 0)
    inside = jnp.logical_and(place >= first, place < last)
    return jnp.sum(jnp.where(inside, depths, 0.0), axis=0, keepdims=True)


def to_column(row):
    return jnp.transpose(jnp.broadcast_to(row, (LANES, row.shape[1])))


def wide(column, width):
    return jnp.concatenate([column] * (width // LANES), axis=1)


def forward_body(
    rays,
    entry_hbm,
    count_hbm,
    step_hbm,
    density_hbm,
    w_first_hbm,
    table_hbm,
    code_hbm,
    w_second_hbm,
    w_feature_hbm,
    keep_ref,
    send_ref,
    depth_ref,
    hidden_one_ref,
    hidden_two_ref,
    mean_hidden_ref,
    w_feature_out_ref,
    logit_ref,
    step_out_ref,
    count_out_ref,
    density_out_ref,
    partial_ref,
    entry_ref,
    w_first_ref,
    table_ref,
    code_ref,
    w_second_ref,
    w_feature_ref,
    done,
):
    cell = lax.axis_index("cell")
    pairs = (
        (w_first_hbm, w_first_ref),
        (table_hbm, table_ref),
        (code_hbm, code_ref),
        (entry_hbm, entry_ref),
        (w_second_hbm, w_second_ref),
        (density_hbm, density_out_ref),
        (count_hbm, count_out_ref),
        (step_hbm, step_out_ref),
        (w_feature_hbm, w_feature_ref),
    )
    copies = [pltpu.make_async_copy(a, b, done.at[i]) for i, (a, b) in enumerate(pairs)]
    for copy in copies:
        copy.start()
    copies[0].wait()
    w_first_t = jnp.transpose(w_first_ref[...].astype(f32)).astype(bf16)
    copies[1].wait()
    rows = table_ref.shape[0]
    table = jnp.concatenate(split_high_low(mm(w_first_t, table_ref[...], NT)), axis=1)
    copies[2].wait()
    code = mm(w_first_t, code_ref[...], NT)
    for copy in copies[3:8]:
        copy.wait()
    w_second_t = jnp.transpose(w_second_ref[...]).astype(bf16)
    density = density_columns(density_out_ref, rays)
    entry = entry_ref[...]
    slot = lax.broadcasted_iota(jnp.int32, (rows, rays), 0)
    for k in range(SAMPLES):
        cols = pl.ds(k * rays, rays)
        hot = (slot == entry + k).astype(f32).astype(bf16)
        hidden_one = jnp.maximum(mm(table, jnp.concatenate([hot, hot], axis=0)) + code, 0.0)
        hidden_one = hidden_one.astype(bf16)
        hidden_one_ref[:, cols] = hidden_one
        hidden_two = jnp.maximum(mm(w_second_t, hidden_one), 0.0).astype(bf16)
        hidden_two_ref[:, cols] = hidden_two
        logit_ref[k : k + 1, :] = jnp.sum(hidden_two.astype(f32) * density, axis=0, keepdims=True)
    depth_steps, weights, _ = slot_scalars(logit_ref[...], step_out_ref[...], count_out_ref[...])
    mean_hidden = jnp.zeros(mean_hidden_ref.shape, f32)
    for k in range(SAMPLES):
        mean_hidden += weights[k] * hidden_two_ref[:, pl.ds(k * rays, rays)].astype(f32)
    mean_hidden_ref[...] = mean_hidden
    copies[8].wait()
    w_feature = w_feature_ref[...].astype(bf16)
    w_feature_out_ref[...] = w_feature
    high, low = split_high_low(jnp.transpose(mean_hidden))
    partial_ref[...] = mm(high, w_feature) + mm(low, w_feature)
    half = keep_ref.shape[0]
    mine = lax.rem(cell, 2)
    keep_ref[...] = partial_ref[pl.ds(pl.multiple_of(mine * half, half), half), :].astype(bf16)
    send_ref[...] = partial_ref[
        pl.ds(pl.multiple_of((1 - mine) * half, half), half), :
    ].astype(bf16)
    place = lax.broadcasted_iota(jnp.int32, depth_ref.shape, 0)
    total = functools.reduce(lambda a, b: a + b, depth_steps)
    depth_ref[...] = jnp.where(place == cell, jnp.broadcast_to(total, depth_ref.shape), 0.0)


def density_columns(density_ref, rays):
    density = density_ref[...].astype(f32)
    return wide(jnp.transpose(jnp.broadcast_to(density, (LANES, density.shape[1]))), rays)


def slot_scalars(logit, step_length, count):
    soft = jnp.maximum(logit, 0.0) + jnp.log1p(jnp.exp(-jnp.abs(logit)))
    depth_steps, weights, behinds = [], [], []
    ahead = jnp.zeros_like(step_length)
    for k in range(SAMPLES):
        travel = jnp.where(k < count, step_length, 0.0)
        depth = soft[k : k + 1, :] * travel
        weights.append(jnp.exp(-ahead) * (1.0 - jnp.exp(-depth)))
        ahead = ahead + depth
        behinds.append(jnp.exp(-ahead))
        depth_steps.append(depth)
    return depth_steps, weights, behinds


def joined(cell, level, rays, mine, theirs, depths, column_ref):
    count = mine.shape[0]
    start = low_start(cell, level)
    fade = jnp.exp(-depth_between(depths, start, start + (1 << level)))
    column_ref[...] = to_column(fade)
    offset = row_offset(cell, level + 1 if count < (rays >> level) else level, rays)
    fade = column_ref[pl.ds(pl.multiple_of(offset, count), count), :]
    is_low = bit_of(cell, level) == 0
    own = wide(jnp.where(is_low, 1.0, fade), mine.shape[1])
    other = wide(jnp.where(is_low, fade, 1.0), mine.shape[1])
    return own * mine.astype(f32) + other * theirs.astype(f32)


def up_body(
    level, rays, mine_ref, theirs_ref, depth_ref, depth_in_ref, keep_ref, send_ref, depth_out_ref,
    column_ref, joined_ref,
):
    cell = lax.axis_index("cell")
    depths = depth_ref[...] + depth_in_ref[...]
    depth_out_ref[...] = depths
    value = joined(cell, level, rays, mine_ref[...], theirs_ref[...], depths, column_ref)
    count, half = value.shape[0], keep_ref.shape[0]
    if half == count:
        keep_ref[...] = value.astype(bf16)
        send_ref[...] = value.astype(bf16)
    else:
        joined_ref[...] = value
        mine = bit_of(cell, level + 1)
        keep_ref[...] = joined_ref[pl.ds(pl.multiple_of(mine * half, half), half), :].astype(bf16)
        send_ref[...] = joined_ref[
            pl.ds(pl.multiple_of((1 - mine) * half, half), half), :
        ].astype(bf16)


def later_light(cell, level, rays, residual, mine, theirs, depths, column_ref):
    count = residual.shape[0]
    high = jnp.where(bit_of(cell, level) == 0, theirs.astype(f32), mine.astype(f32))
    dots = jnp.sum(high * residual, axis=1, keepdims=True)
    offset = row_offset(cell, level if count == (rays >> level) else level + 1, rays)
    column_ref[...] = jnp.zeros_like(column_ref)
    column_ref[pl.ds(pl.multiple_of(offset, count), count), :] = jnp.broadcast_to(
        dots, (count, LANES)
    )
    row = jnp.transpose(column_ref[...])[0:1, :]
    transmit = jnp.exp(-depth_between(depths, 0, low_start(cell, level) + (1 << level)))
    return transmit * row


def share_light(cell, level, later, light, own_ref, their_ref):
    is_low = bit_of(cell, level) == 0
    own_ref[...] = jnp.broadcast_to(later + jnp.where(is_low, light, 0.0), own_ref.shape)
    their_ref[...] = jnp.broadcast_to(later + jnp.where(is_low, 0.0, light), their_ref.shape)


def top_body(
    level, rays, mine_ref, theirs_ref, depth_ref, depth_in_ref, under_mine_ref, under_theirs_ref,
    target_ref, color_ref, later_ref, later_send_ref, depth_out_ref, column_ref,
):
    cell = lax.axis_index("cell")
    depths = depth_ref[...] + depth_in_ref[...]
    depth_out_ref[...] = depths
    mine, theirs = mine_ref[...], theirs_ref[...]
    color = joined(cell, level, rays, mine, theirs, depths, column_ref).astype(bf16)
    color_ref[...] = color
    count = color.shape[0]
    offset = pl.multiple_of(row_offset(cell, level, rays), count)
    residual = color.astype(f32) - target_ref[pl.ds(offset, count), :].astype(f32)
    light = later_light(cell, level, rays, residual, mine, theirs, depths, column_ref)
    later = jnp.where(bit_of(cell, level) == 0, light, 0.0)
    light = later_light(
        cell, level - 1, rays, residual, under_mine_ref[...], under_theirs_ref[...], depths,
        column_ref,
    )
    share_light(cell, level - 1, later, light, later_ref, later_send_ref)


def assembled(cell, level, mine, theirs, out_ref):
    count = mine.shape[0]
    bit = bit_of(cell, level)
    out_ref[pl.ds(pl.multiple_of(bit * count, count), count), :] = mine
    out_ref[pl.ds(pl.multiple_of((1 - bit) * count, count), count), :] = theirs


def down_body(
    level, rays, color_ref, color_in_ref, later_ref, later_in_ref, depth_ref, mine_ref, theirs_ref,
    target_ref, color_out_ref, later_out_ref, later_send_ref, column_ref,
):
    cell = lax.axis_index("cell")
    assembled(cell, level + 1, color_ref[...], color_in_ref[...], color_out_ref)
    later = later_ref[0:1, :] + later_in_ref[0:1, :]
    count = color_out_ref.shape[0]
    offset = pl.multiple_of(row_offset(cell, level + 1, rays), count)
    residual = color_out_ref[...].astype(f32) - target_ref[pl.ds(offset, count), :].astype(f32)
    light = later_light(
        cell, level, rays, residual, mine_ref[...], theirs_ref[...], depth_ref[...], column_ref
    )
    share_light(cell, level, later, light, later_out_ref, later_send_ref)


def feature_body(
    rays,
    color_ref,
    color_in_ref,
    later_ref,
    later_in_ref,
    depth_ref,
    target_ref,
    mean_hidden_ref,
    whole_ref,
    grad_depth_ref,
    residual_ref,
    transmit_ref,
    *grad_refs,
):
    cell = lax.axis_index("cell")
    grad_depth_ref[...] = -(later_ref[...] + later_in_ref[...])
    assembled(cell, 0, color_ref[...], color_in_ref[...], whole_ref)
    color = whole_ref[...]
    residual = (color.astype(f32) - target_ref[...].astype(f32)).astype(bf16)
    transmit = jnp.exp(-depth_between(depth_ref[...], 0, cell))
    seen = (mean_hidden_ref[...] * transmit).astype(bf16)
    start = 0
    for ref in grad_refs:
        ref[...] = mm(seen, residual[:, start : start + ref.shape[1]]).astype(bf16)
        start += ref.shape[1]
    residual_ref[...] = residual
    transmit_ref[...] = jnp.broadcast_to(transmit, transmit_ref.shape)


def output_body(color_ref, grad_depth_ref, rendered_ref, depth_grad_ref):
    cell = lax.axis_index("cell")
    width, channels = rendered_ref.shape[0], color_ref.shape[1]
    place = lax.broadcasted_iota(jnp.int32, (width, channels), 0)
    channel = lax.broadcasted_iota(jnp.int32, (width, channels), 1)
    chosen = (channel == place + cell * width).astype(f32).astype(bf16)
    rendered_ref[...] = mm(chosen, color_ref[...], NT).astype(bf16)
    depth_grad_ref[...] = grad_depth_ref[0:1, :]


def hidden_body(
    rays,
    w_feature_ref,
    residual_ref,
    transmit_ref,
    grad_depth_ref,
    hidden_one_ref,
    hidden_two_ref,
    logit_ref,
    step_ref,
    count_ref,
    density_ref,
    second_ref,
):
    hidden = hidden_one_ref.shape[0]
    pulled = mm(w_feature_ref[...], residual_ref[...], NT) * transmit_ref[0:1, :]
    grad_depth = grad_depth_ref[0:1, :]
    logit = logit_ref[...]
    _, weights, behinds = slot_scalars(logit, step_ref[...], count_ref[...])
    small = jnp.exp(-jnp.abs(logit))
    sigmoid = jnp.where(logit >= 0.0, 1.0, small) / (1.0 + small)
    dots = [
        jnp.sum(hidden_two_ref[:, pl.ds(k * rays, rays)].astype(f32) * pulled, axis=0, keepdims=True)
        for k in range(SAMPLES)
    ]
    later = jnp.zeros_like(grad_depth)
    grad_logits = [None] * SAMPLES
    for k in reversed(range(SAMPLES)):
        grad_step = behinds[k] * dots[k] - later + grad_depth
        later = later + weights[k] * dots[k]
        travel = jnp.where(k < count_ref[...], step_ref[...], 0.0)
        grad_logits[k] = grad_step * travel * sigmoid[k : k + 1, :]
    density = density_columns(density_ref, rays)
    grad_second = jnp.zeros((hidden, hidden), f32)
    for k in range(SAMPLES):
        cols = pl.ds(k * rays, rays)
        grad_hidden = weights[k] * pulled + grad_logits[k] * density
        grad_before = jnp.where(hidden_two_ref[:, cols].astype(f32) > 0, grad_hidden, 0.0)
        grad_second += mm(hidden_one_ref[:, cols], grad_before.astype(bf16), NT)
    second_ref[...] = grad_second.astype(bf16)


def add_body(a_ref, b_ref, out_ref):
    out_ref[...] = (a_ref[...].astype(f32) + b_ref[...].astype(f32)).astype(out_ref.dtype)


def square_body(a_ref, b_ref, *rest):
    *before_ref, out_ref, sum_ref = rest
    value = a_ref[...].astype(f32) + b_ref[...].astype(f32)
    out_ref[...] = value
    total = jnp.sum(jnp.sum(value * value, axis=0, keepdims=True), axis=1, keepdims=True)
    total = jnp.broadcast_to(total, sum_ref.shape)
    sum_ref[...] = total + before_ref[0][...] if before_ref else total


def adam_of(gradient, mean_moment, square_moment, rescale):
    unit_grad = gradient * rescale
    mean_new = (beta_first / bias_first) * mean_moment + ((1.0 - beta_first) / bias_first) * unit_grad
    square_new = (beta_second / bias_second) * square_moment + (
        (1.0 - beta_second) / bias_second
    ) * (unit_grad * unit_grad)
    return (mean_new / (square_new * lax.rsqrt(square_new) + adam_floor)).astype(bf16)


def adam_body(entries, sum_ref, sum_in_ref, *rest):
    *in_refs, update_second_hbm, update_feature_hbm, second_ref, feature_ref, done = rest
    *grad_refs, mean_second_ref, square_second_ref, mean_feature_ref, square_feature_ref = in_refs
    *part_refs, last_ref = grad_refs
    rescale = lax.rsqrt((sum_ref[0:1, :] + sum_in_ref[0:1, :]) / entries + mean_floor)
    block = feature_ref.shape[0] // ADAM_BLOCKS
    copies = []
    for i in range(ADAM_BLOCKS):
        rows = pl.ds(i * block, block)
        start = 0
        for ref in part_refs:
            cols = pl.ds(start, ref.shape[1])
            feature_ref[rows, cols] = adam_of(
                ref[rows, :], mean_feature_ref[rows, cols], square_feature_ref[rows, cols],
                wide(rescale, ref.shape[1]),
            )
            start += ref.shape[1]
        second_ref[rows, :] = adam_of(
            last_ref[rows, :], mean_second_ref[rows, :], square_second_ref[rows, :],
            wide(rescale, second_ref.shape[1]),
        )
        for j, (value, out) in enumerate(
            ((feature_ref, update_feature_hbm), (second_ref, update_second_hbm))
        ):
            copy = pltpu.make_async_copy(value.at[rows], out.at[rows], done.at[i, j])
            copy.start()
            copies.append(copy)
    for copy in copies:
        copy.wait()


def swap(value, axis, bit):
    count = lax.axis_size(axis)
    return lax.ppermute(value, axis, [(i, i ^ (1 << bit)) for i in range(count)])


def swap_cells(value, flip):
    count = lax.axis_size("cell")
    return lax.ppermute(value, "cell", [(i, i ^ flip) for i in range(count)])


def swap_groups(value, turn):
    cells, groups = lax.axis_size("cell"), lax.axis_size("rays")
    spread = groups.bit_length() - 1
    pairs = [
        (c * groups + g, c * groups + (g ^ (1 << ((turn + c) % spread))))
        for c in range(cells)
        for g in range(groups)
    ]
    return lax.ppermute(value, ("cell", "rays"), pairs)


def on_device(
    ray_code,
    entry_index,
    sample_count,
    step_length,
    positions,
    w_first,
    w_second,
    w_density,
    w_feature,
    mean_second,
    square_second,
    mean_feature,
    square_feature,
    target_color,
):
    rays, _, hidden = ray_code.shape
    features = w_feature.shape[2]
    cells = lax.axis_size("cell")
    groups = lax.axis_size("rays")
    levels = cells.bit_length() - 1
    spread = groups.bit_length() - 1
    entry, count, step = entry_index.T, sample_count.T, step_length.T
    column = pltpu.VMEM((rays, LANES), f32)

    half = rays // 2
    (
        keep, send, depths, hidden_one, hidden_two, mean_hidden, w_feature_b, logit, step, count,
        density,
    ) = kernel_call(
        functools.partial(forward_body, rays),
        [
            ((half, features), bf16),
            ((half, features), bf16),
            ((cells, rays), f32),
            ((hidden, SAMPLES * rays), bf16),
            ((hidden, SAMPLES * rays), bf16),
            ((hidden, rays), f32),
            ((hidden, features), bf16),
            ((SAMPLES, rays), f32),
            (step.shape, f32),
            (count.shape, jnp.int32),
            (w_density.shape, bf16),
        ],
        [
            pltpu.VMEM((rays, features), f32),
            pltpu.VMEM(entry.shape, jnp.int32),
            pltpu.VMEM(w_first.shape[1:], bf16),
            pltpu.VMEM(positions.shape[1:], bf16),
            pltpu.VMEM((rays, hidden), bf16),
            pltpu.VMEM(w_second.shape[1:], f32),
            pltpu.VMEM(w_feature.shape[1:], f32),
            pltpu.SemaphoreType.DMA((9,)),
        ],
        "forward",
        16,
        pltpu.HBM,
    )(entry, count, step, w_density, w_first[0], positions[0], ray_code[:, 0, :], w_second[0],
      w_feature[0])

    held = []
    for level in range(levels - 1):
        theirs = swap(send, "cell", level)
        depths_in = swap(depths, "cell", level)
        held.append((keep, theirs))
        rows = keep.shape[0]
        next_rows = rows if level == levels - 2 else rows // 2
        keep, send, depths = kernel_call(
            functools.partial(up_body, level, rays),
            [((next_rows, features), bf16), ((next_rows, features), bf16), ((cells, rays), f32)],
            [column, pltpu.VMEM((rows, features), f32)],
            f"up_{level}",
        )(keep, theirs, depths, depths_in)

    theirs = swap(send, "cell", levels - 1)
    depths_in = swap(depths, "cell", levels - 1)
    color, later, later_send, depths = kernel_call(
        functools.partial(top_body, levels - 1, rays),
        [(keep.shape, bf16), ((8, rays), f32), ((8, rays), f32), ((cells, rays), f32)],
        [column],
        "top",
    )(keep, theirs, depths, depths_in, *held[-1], target_color)

    for level in reversed(range(levels - 2)):
        color_in = swap(color, "cell", level + 1)
        later_in = swap(later_send, "cell", level + 1)
        color, later, later_send = kernel_call(
            functools.partial(down_body, level, rays),
            [((2 * color.shape[0], features), bf16), ((8, rays), f32), ((8, rays), f32)],
            [column],
            f"down_{level}",
        )(color, color_in, later, later_in, depths, *held[level], target_color)

    color_in = swap(color, "cell", 0)
    later_in = swap(later_send, "cell", 0)
    part = (hidden, features // FEATURE_PARTS)
    whole, grad_depth, residual, transmit, *grads = kernel_call(
        functools.partial(feature_body, rays),
        [((rays, features), bf16), ((8, rays), f32), ((rays, features), bf16), ((8, rays), f32)]
        + [(part, bf16)] * FEATURE_PARTS,
        (),
        "feature",
    )(color, color_in, later, later_in, depths, target_color, mean_hidden)
    grads += kernel_call(
        functools.partial(hidden_body, rays), [((hidden, hidden), bf16)], (), "hidden", 12
    )(w_feature_b, residual, transmit, grad_depth, hidden_one, hidden_two, logit, step, count, density)
    rendered, depth_grad = kernel_call(
        output_body, [((features // cells, rays), bf16), ((1, rays), f32)], (), "outputs"
    )(whole, grad_depth)

    total = ()
    for turn in range(spread):
        arrived = [swap_groups(grad, turn) for grad in grads]
        for i, (grad, other) in enumerate(zip(grads, arrived)):
            if turn < spread - 1:
                (grads[i],) = kernel_call(add_body, [(grad.shape, bf16)], (), f"add_{i}")(
                    grad, other
                )
            else:
                grads[i], *total = kernel_call(
                    square_body, [(grad.shape, f32), ((8, LANES), f32)], (), f"square_{i}"
                )(grad, other, *total)
    (total,) = total

    beside, above, across = (swap_cells(total, flip) for flip in (1, 2, 3))
    total = (total + beside) + (above + across)
    for level in range(2, levels):
        total_in = swap_cells(total, 1 << level | 1)
        if level < levels - 1:
            total = total + total_in

    entries = cells * (hidden * features + hidden * hidden)
    update_second, update_feature = kernel_call(
        functools.partial(adam_body, entries),
        [((hidden, hidden), bf16), ((hidden, features), bf16)],
        [
            pltpu.VMEM((hidden, hidden), bf16),
            pltpu.VMEM((hidden, features), bf16),
            pltpu.SemaphoreType.DMA((ADAM_BLOCKS, 2)),
        ],
        "adam",
        out_space=pltpu.HBM,
    )(total, total_in, *grads, mean_second[0], square_second[0], mean_feature[0],
      square_feature[0])
    return (rendered.T, depth_grad.T, update_second[None], update_feature[None])


def solution(mesh):
    in_specs = (
        P("rays", "cell", None),
        P("rays", "cell"),
        P("rays", "cell"),
        P("rays", "cell"),
        P("cell", None, None),
        P("cell", None, None),
        P("cell", None, None),
        P("cell", None),
        P("cell", None, None),
        P("cell", None, None),
        P("cell", None, None),
        P("cell", None, None),
        P("cell", None, None),
        P("rays", None),
    )
    out_specs = (P("rays", "cell"), P("rays", "cell"), P("cell", None, None), P("cell", None, None))
    return jax.shard_map(
        on_device, mesh=mesh, in_specs=in_specs, out_specs=out_specs, check_vma=False
    )
```
